32 devices in a mesh: space: 4 (over y, x), slot: 8 (over z, core).
Axes of the slice: x: 2, y: 2, z: 4, core: 2. Of those that a mesh axis runs over, the one named last changes fastest.
Arguments:
- control: bfloat16 [1536, 1024], P('slot', 'space'), may hold values from -6 to 6
- block_lists: int32 [32, 2], P('space'), may hold values from 0 to 7, all different within a row; in each aligned block of 8 rows (0 to 7, 8 to 15, ...) at most 2 rows name the same one
- loc_tiles: bfloat16 [32, 2, 128, 128], P('space'), may hold values from -0.375 to 0.375
- ensemble: bfloat16 [8, 1536, 4096], P('slot', None, 'space'), may hold values from -2.5 to 2.5
- obs_col: int32 [8, 8192], P('slot', 'space'), may hold values from 0 to 4095, as said below
- obs_wts: float32 [8, 48, 8192], P('slot', None, 'space'), may hold values from -0.875 to 0.875
- innovation: float32 [8, 8192], P('slot', 'space'), may hold values from -6 to 6
- inv_error: float32 [8, 8192], P('slot', 'space'), may hold values from 1 to 16
Outputs:
- first_grad: float32 [1536, 1024], P('slot', 'space')
- second_grad: float32 [1536, 1024], P('slot', 'space')
The draws below stay inside these ranges and needn't reach their ends.
Inputs may be any that keep to these rules, and one draw needn't show every extreme that they name: `block_lists`: each grid block lists 2 different control blocks; among the grid blocks of one space index no control block is listed more than twice. `obs_col`: observation j lies in grid columns (j // 2048) * 8 * 128 to that plus 8 * 128 - 1.
All inputs are finite; a program needn't handle non-finite values.
Results may differ from the reference program's by a relative error of at most 0.0003.
Values may be sent and summed in bfloat16 or wider, within the bound.
A program may use at most 64 MiB of HBM per device.

```python
import math
import jax
import jax.numpy as jnp
import numpy as np
from jax import lax

LEV = 48
MEMBERS = 32
BLOCK = 128
K = 2
NOBS_DEV = 2048
GB_DEV = 8
SLOTS = 8
COLS = 1536
NCB = 8
NC = 1024
NGB = 32
NG = 4096
NOBS = 8192


def draw_obs_col(key, part):
    offsets = jax.random.randint(key, (SLOTS, NOBS), 0, GB_DEV * BLOCK, dtype=jnp.int32)
    offsets = offsets.at[:, 0].set(0)
    offsets = offsets.at[:, NOBS - 1].set(GB_DEV * BLOCK - 1)
    owner = jnp.arange(NOBS, dtype=jnp.int32) // NOBS_DEV
    return (offsets + owner[None, :] * (GB_DEV * BLOCK)).astype(jnp.int32)


def shard_levels(own_key, dims, pieces, least, largest):
    def one(position, parts):
        draws = jax.random.uniform(jax.random.fold_in(jax.random.fold_in(own_key, 6), position), (parts,), jnp.float32, least / len(pieces), largest / len(pieces))
        return jnp.repeat(jnp.exp(draws), dims[position] // parts).reshape((-1,) + (1,) * (len(dims) - position - 1))

    factor_of = one(*pieces[0])
    for cut in pieces[1:]:
        factor_of = factor_of * one(*cut)
    return factor_of


def shared_out(own_key, own, number, rows, amount, top, bound, skew):
    ranking = jax.random.permutation(own_key, amount)
    heavy_load, ordinary = load_shares(amount, rows * top, bound, skew, True), load_shares(amount, rows * top, bound, skew, False)
    places = jnp.arange(amount)

    def named(lengths, rotation):
        used = int((lengths > 0).sum())
        fixed = max(1, used // 4)
        passed = fixed + (places - fixed + rotation * (used - fixed)) % max(1, amount - fixed)
        return jnp.zeros((amount,), jnp.int32).at[ranking[jnp.where(places < fixed, places, passed)]].set(jnp.asarray(lengths, jnp.int32))

    lengths = jnp.where(number % 4 == 0, named(heavy_load, number // 4), named(ordinary, number - number // 4 - 1))
    mixed = jax.random.permutation(jax.random.fold_in(own, 3), amount)
    donor, taker = mixed[0:amount // 2 * 2:2], mixed[1:amount // 2 * 2:2]
    margin = jnp.minimum(lengths[donor] - 1, bound - lengths[taker]) // 2
    margin = jnp.where((donor == ranking[0]) | (taker == ranking[0]) | (lengths[taker] == 0), 0, jnp.maximum(margin, 0))
    passed = jax.random.randint(jax.random.fold_in(own, 4), (amount // 2,), 0, 1 << 20) % (margin + 1)
    lengths = lengths.at[donor].add(-passed).at[taker].add(passed)
    labels = jnp.searchsorted(jnp.cumsum(lengths), jnp.arange(rows * top), side="right").astype(jnp.int32)
    grid = labels.reshape(top, rows).T
    grid = grid[jax.random.permutation(jax.random.fold_in(own, 1), rows)]
    rotation = jax.random.randint(jax.random.fold_in(own, 2), (rows, 1), 0, top)
    return jnp.take_along_axis(grid, (jnp.arange(top)[None, :] + rotation) % top, axis=1)


def load_shares(amount, total, reach, skew, full):
    loads = [(1 << 20) // math.isqrt(grade ** skew) + 1 for grade in range(1, amount + 1)]
    largest = reach if full else min(reach, max(-(-total // amount), total * loads[0] // sum(loads)))
    least = 1 if total - largest >= amount - 1 else 0
    given, surplus = [largest] + [least] * (amount - 1), total - largest - least * (amount - 1)
    while surplus > 0:
        free = [i for i in range(1, amount) if given[i] < largest] or [i for i in range(1, amount) if given[i] < reach]
        mass, remaining = sum([loads[i] for i in free]), surplus
        for i in free:
            more = min(reach - given[i], max(1, remaining * loads[i] // mass), surplus)
            given[i] = given[i] + more
            surplus = surplus - more
    return np.array(given)


def gaussian(own_key, shape, deviation, limit, split=(), kind=jnp.bfloat16):
    drawn = deviation * jax.random.normal(own_key, shape, jnp.float32)
    if split:
        drawn = drawn * shard_levels(own_key, shape, split, -0.22, 0.18)
    return jnp.clip(drawn, -limit, limit).astype(kind)


def setup_inputs(seed: int = 0) -> dict:
    keys = jax.random.split(jax.random.key(seed), 9)
    control = gaussian(keys[0], (COLS, NC), 1.0, 6.0, ((0, 8), (1, 4)))
    block_lists_keys = jax.random.split(jax.random.fold_in(keys[1], 1), NGB // GB_DEV)
    block_lists_turns = jax.random.permutation(jax.random.fold_in(keys[1], 3), NGB // GB_DEV)
    block_lists = jax.vmap(lambda own, number: shared_out(jax.random.fold_in(keys[1], 2), own, number, GB_DEV, NCB, K, 2, 2))(block_lists_keys, block_lists_turns).reshape((NGB, K))
    loc_tiles = gaussian(keys[2], (NGB, K, BLOCK, BLOCK), (BLOCK * K) ** -0.5, 0.375, ((0, 4),))
    ensemble = gaussian(keys[3], (SLOTS, COLS, NG), 0.18, 2.5, ((0, 8), (2, 4)))
    obs_col = draw_obs_col(jax.random.fold_in(keys[8], 71), 0)
    obs_wts = gaussian(keys[5], (SLOTS, LEV, NOBS), LEV ** -0.5, 0.875, ((0, 8), (2, 4)), jnp.float32)
    innovation = gaussian(keys[6], (SLOTS, NOBS), 1.0, 6.0, ((0, 8), (1, 4)), jnp.float32)
    inv_error = jnp.clip(jnp.exp(math.log(16.0) - 2.7725887 * jax.random.uniform(keys[7], (SLOTS, NOBS), jnp.float32) ** shard_levels(keys[7], (SLOTS, NOBS), ((0, 8), (1, 4)), -0.2, 0.2)), 1.0, 16.0)
    return dict(control=control, block_lists=block_lists, loc_tiles=loc_tiles, ensemble=ensemble, obs_col=obs_col, obs_wts=obs_wts, innovation=innovation, inv_error=inv_error)


descent_step = 0.5


def localize(control, block_lists, loc_tiles):
    picked = control.astype(jnp.float32).reshape(COLS, NCB, BLOCK)[:, block_lists.reshape(-1), :]
    tiles_flat = loc_tiles.reshape(NGB * K, BLOCK, BLOCK).astype(jnp.float32)
    products = jnp.einsum("crj,rij->cri", picked, tiles_flat, precision=lax.Precision.HIGHEST)
    return products.reshape(COLS, NGB, K, BLOCK).sum(axis=2).reshape(COLS, NG)


def adjoint(forcing, block_lists, loc_tiles):
    grid_cells = forcing.reshape(COLS, NGB, BLOCK)
    products = jnp.einsum("cgi,gkij->cgkj", grid_cells, loc_tiles.astype(jnp.float32), precision=lax.Precision.HIGHEST)
    selector = (block_lists.reshape(-1)[:, None] == jnp.arange(NCB, dtype=jnp.int32)[None, :]).astype(jnp.float32)
    summed = jnp.einsum("rb,crj->cbj", selector, products.reshape(COLS, NGB * K, BLOCK), precision=lax.Precision.HIGHEST)
    return summed.reshape(COLS, NC)


def gradient(control, block_lists, loc_tiles, ensemble, obs_col, obs_wts, innovation, inv_error):
    updates = localize(control, block_lists, loc_tiles).reshape(MEMBERS, LEV, NG)

    def slot_step(running, slot_items):
        members, columns, weights, observed, inverse = slot_items
        spread = members.astype(jnp.float32).reshape(MEMBERS, LEV, NG)
        increment = jnp.sum(spread * updates, axis=0)
        modelled = jnp.sum(weights * increment[:, columns], axis=0)
        residual = inverse * (modelled - observed)
        adjoint_obs = jnp.zeros((LEV, NG), jnp.float32).at[:, columns].add(weights * residual[None, :])
        return running + (spread * adjoint_obs[None]).reshape(COLS, NG), None

    forcing, unused = lax.scan(slot_step, jnp.zeros((COLS, NG), jnp.float32), (ensemble, obs_col, obs_wts, innovation, inv_error))
    return control.astype(jnp.float32) + adjoint(forcing, block_lists, loc_tiles)


def reference(control, block_lists, loc_tiles, ensemble, obs_col, obs_wts, innovation, inv_error):
    first_grad = gradient(control, block_lists, loc_tiles, ensemble, obs_col, obs_wts, innovation, inv_error)
    stepped = control.astype(jnp.float32) - descent_step * first_grad
    second_grad = gradient(stepped, block_lists, loc_tiles, ensemble, obs_col, obs_wts, innovation, inv_error)
    return first_grad, second_grad
```

```python
import functools

import jax
import jax.numpy as jnp
from jax import lax
from jax.experimental import pallas as pl
from jax.experimental.pallas import tpu as pltpu
from jax.sharding import PartitionSpec as P

LEV = 48
BLOCK = 128
CORES = 2
OBS_CHUNK = 512
PAD = 16
TOP = 32700.0
FINE = 256.0
descent_step = 0.5
F32 = jnp.float32
BF16 = jnp.bfloat16
I16 = jnp.int16
I32 = jnp.int32
MESH = pl.DeviceIdType.MESH


def halves(x):
    high = x.astype(BF16)
    return high, (x - high.astype(F32)).astype(BF16)


def dot(a, b):
    return lax.dot_general(a, b, (((1,), (0,)), ((), ())), preferred_element_type=F32)


def tree(spaces, chips, per):
    hops, children = {}, {}
    for j in range(per):
        for m in range(spaces):
            for k in range(chips):
                if not m and not k:
                    continue
                along_space = m if j % 2 == 0 else not k
                if along_space:
                    bits = [1 << i for i in range(spaces.bit_length()) if m >> i & 1]
                    bit = bits[(k + j) % len(bits)]
                    hops[m, k, j] = ("space", bit)
                    above = (m ^ bit, k, j)
                else:
                    if 2 * k == chips:
                        step = 1 if (m + j) % 2 == 0 else -1
                    else:
                        step = 1 if 2 * k < chips else -1
                    hops[m, k, j] = ("z", step)
                    above = (m, (k - step) % chips, j)
                children.setdefault(above, []).append((m, k, j))
    return hops, children


def distance(message, chips):
    m, k, j = message
    return bin(m).count("1") + min(k, chips - k)


def encode(x, ref, slot, rows):
    top = jnp.max(jnp.abs(x), axis=0, keepdims=True)
    log = jnp.ceil(jnp.log2(jnp.maximum(top, 1e-36)) * FINE)
    log = jnp.clip(log, -126.0 * FINE, 126.0 * FINE)
    scale = jnp.exp2(log * (1.0 / FINE)) * (1.0 / TOP)
    ref[slot, :rows] = jnp.round(x * (1.0 / scale)).astype(I32).astype(I16)
    ref[slot, rows : rows + PAD] = jnp.broadcast_to(log, (PAD, BLOCK)).astype(I32).astype(I16)


def decode(ref, slot, rows):
    log = ref[slot, rows : rows + PAD].astype(I32).astype(F32)[:1]
    scale = jnp.exp2(log * (1.0 / FINE)) * (1.0 / TOP)
    return ref[slot, :rows].astype(I32).astype(F32) * scale


def kernel(spaces, slots, *refs):
    chips = slots // CORES
    (control, lists, tiles, ensemble, cols, wts, innovation, inverse, first_ref, second_ref) = refs[:10]
    ctl, coded = refs[10 : 10 + chips], refs[10 + chips : 10 + 2 * chips]
    (
        ens, tiles_t, tiles_a, inv, pick, pick_t, inc, inc_out, inc_in, pair, adj, adj_in, split, forced, con, step,
        rs_out, rs_in, own_s, ens_s, ens_r, ag_s, ag_r, rs_s, rs_r, x_s, x_r,
    ) = refs[10 + 2 * chips :]
    rows, width = control.shape
    per = width // BLOCK
    cells = ensemble.shape[2]
    nobs = cols.shape[1]
    blocks = cells // BLOCK
    listed = lists.shape[1]
    ncb = spaces * per
    members = rows // LEV
    me = lax.axis_index("space")
    slot = lax.axis_index("slot")
    z, core = slot // CORES, lax.rem(slot, CORES)
    sibling = {"slot": slot + 1 - 2 * core}
    hops, children = tree(spaces, chips, per)

    def space_at(m):
        at, i = me, 1
        while i < spaces:
            if m & i:
                at = at + i * (1 - 2 * lax.rem(me // i, 2))
            i *= 2
        return at

    def slot_at(dz):
        return lax.rem(z + dz + chips, chips) * CORES + core

    def number(message):
        m, k, j = message
        return (j * spaces + m) * chips + k

    barrier = pltpu.get_barrier_semaphore()
    near = [{"space": space_at(1 << i)} for i in range(spaces.bit_length() - 1)]
    near += [{"slot": slot_at(1)}, {"slot": slot_at(-1)}, sibling]
    for where in near:
        pl.semaphore_signal(barrier, inc=1, device_id=where, device_id_type=MESH)
    pl.semaphore_wait(barrier, len(near))

    started = []

    def send(src, dst, ssem, rsem, where):
        copy = pltpu.make_async_remote_copy(
            src_ref=src, dst_ref=dst, send_sem=ssem, recv_sem=rsem,
            device_id=where, device_id_type=MESH,
        )
        copy.start()
        started.append(copy)
        return copy

    gathers = {}

    def pass_on(i, message):
        m, k, j = message
        held = coded if i else ctl
        at = per * space_at(m) + j
        for child in children.get(message, []):
            kind, hop = hops[child]
            where = {"space": space_at(hop)} if kind == "space" else {"slot": slot_at(-hop)}
            to = number(child)
            gathers[i, child] = send(
                held[k].at[at], held[child[1]].at[at], ag_s.at[i, to], ag_r.at[i, to], where
            )

    def relay(i, depth):
        for message in hops:
            if distance(message, chips) == depth:
                gathers[i, message].wait_recv()
                pass_on(i, message)

    for j in range(per):
        ctl[0][per * me + j] = control[:, j * BLOCK : (j + 1) * BLOCK]
    for j in range(per):
        pass_on(0, (0, 0, j))
    moved = []
    for k in range(chips):
        there = lax.rem(z + k, chips) * CORES
        moved.append(send(ensemble.at[there + 1 - core], ens.at[1, k], ens_s.at[k], ens_r.at[k], sibling).wait_recv)
        own = pltpu.make_async_copy(ensemble.at[there + core], ens.at[0, k], own_s.at[k])
        own.start()
        moved.append(own.wait)

    def build_tiles(g, carry):
        for e in range(listed):
            tiles_t[g, e * BLOCK : (e + 1) * BLOCK] = tiles[g, e].astype(F32).T.astype(BF16)
        return carry

    lax.fori_loop(0, blocks, build_tiles, 0)

    def build_adjoint(b, carry):
        one, two = jnp.int32(-1), jnp.int32(-1)
        for g in range(blocks):
            for e in range(listed):
                hit = lists[g, e] == b
                two = jnp.where(hit, jnp.where(one >= 0, g * listed + e, two), two)
                one = jnp.where(hit, jnp.where(one >= 0, one, g * listed + e), one)
        for place, found in enumerate((one, two)):
            kept = jnp.where(found >= 0, 1.0, 0.0)
            found = jnp.maximum(found, 0)
            g = found // listed
            inv[b, place] = g
            tile = tiles[g, lax.rem(found, listed)].astype(F32) * kept
            tiles_a[b, place * BLOCK : (place + 1) * BLOCK] = tile.astype(BF16)
        return carry

    lax.fori_loop(0, ncb, build_adjoint, 0)

    first_cell = me * cells

    def build_pick(q):
        line = cols[:, q * OBS_CHUNK : (q + 1) * OBS_CHUNK] - first_cell

        def band(r, carry):
            rowid = lax.broadcasted_iota(I32, (BLOCK, OBS_CHUNK), 0) + r * BLOCK
            at = pl.ds(pl.multiple_of(r * BLOCK, BLOCK), BLOCK)
            pick[q, at] = jnp.where(rowid == line, 1.0, 0.0).astype(BF16)
            return carry

        lax.fori_loop(0, blocks, band, 0)
        turned = [
            jnp.broadcast_to(line[:, h * BLOCK : (h + 1) * BLOCK].astype(F32), (BLOCK, BLOCK)).T
            for h in range(OBS_CHUNK // BLOCK)
        ]

        def band_t(r, carry):
            lane = (lax.broadcasted_iota(I32, (BLOCK, BLOCK), 1) + r * BLOCK).astype(F32)
            at = pl.ds(pl.multiple_of(r * BLOCK, BLOCK), BLOCK)
            for h, column in enumerate(turned):
                pick_t[q, h * BLOCK : (h + 1) * BLOCK, at] = jnp.where(column == lane, 1.0, 0.0).astype(BF16)
            return carry

        lax.fori_loop(0, blocks, band_t, 0)

    def member(n):
        return slice(n * LEV, (n + 1) * LEV)

    def lanes(g):
        return pl.ds(pl.multiple_of(g * BLOCK, BLOCK), BLOCK)

    def spread(i, k, fresh):
        if i:

            def unpack(b, carry):
                up, down = halves(decode(coded[k], b, rows))
                split[b, :rows] = up
                split[b, rows:] = down
                return carry

            lax.fori_loop(0, ncb, unpack, 0)

        def run(g, carry):
            held = split if i else ctl[k]
            left = jnp.concatenate([held[lists[g, e]] for e in range(listed)], axis=1)
            value = dot(left, tiles_t[g])
            if i:
                value = value[:rows] + value[rows:]
            at = lanes(g)
            for s, target in enumerate((inc, inc_out.at[i])):
                total = None if fresh else target[:, at]
                for n in range(members):
                    term = ens[s, k, member(n), at].astype(F32) * value[member(n)]
                    total = term if total is None else total + term
                target[:, at] = total
            return carry

        lax.fori_loop(0, blocks, run, 0)

    def observe_all(i):
        swap = send(inc_out.at[i], inc_in.at[i], x_s.at[i, 0], x_r.at[i, 0], sibling)
        swap.wait_recv()
        high, low = halves(inc[...] + inc_in[i])
        pair[:LEV] = high
        pair[LEV:] = low
        adj[i] = jnp.zeros((LEV, cells), F32)

        def observe(q, carry):
            at = pl.ds(pl.multiple_of(q * OBS_CHUNK, OBS_CHUNK), OBS_CHUNK)
            seen = dot(pair[...], pick[q])
            seen = seen[:LEV] + seen[LEV:]
            w = wts[0, :, at]
            modelled = jnp.sum(w * seen, axis=0, keepdims=True)
            residual = inverse[:, at] * (modelled - innovation[:, at])
            up, down = halves(w * residual)
            back = dot(jnp.concatenate([up, down], axis=0), pick_t[q])
            adj[i] += back[:LEV] + back[LEV:]
            return carry

        lax.fori_loop(0, nobs // OBS_CHUNK, observe, 0)
        swap = send(adj.at[i], adj_in.at[i], x_s.at[i, 1], x_r.at[i, 1], sibling)
        swap.wait_recv()

    def force(i, k):
        def fill(g, carry):
            at = lanes(g)
            mine, other = adj[i, :, at], adj_in[i, :, at]
            for n in range(members):
                total = ens[0, k, member(n), at].astype(F32) * mine + ens[1, k, member(n), at].astype(F32) * other
                up, down = halves(total)
                forced[g, member(n)] = up
                forced[g, rows + n * LEV : rows + (n + 1) * LEV] = down
            return carry

        lax.fori_loop(0, blocks, fill, 0)

        def multiply(b, carry):
            left = jnp.concatenate([forced[inv[b, place]] for place in range(2)], axis=1)
            both = dot(left, tiles_a[b])
            con[k, b] = both[:rows] + both[rows:]
            return carry

        lax.fori_loop(0, ncb, multiply, 0)

    sums, used = {}, {}

    def partial(i, message):
        m, k, j = message
        total = con[k, per * space_at(m) + j]
        for child in children.get(message, []):
            sums[i, child].wait_recv()
            total = total + decode(rs_in, number(child), rows)
        return total

    def pass_up(i, message):
        kind, hop = hops[message]
        at = number(message)
        total = partial(i, message)
        if message in used:
            used[message].wait_send()
            started[:] = [copy for copy in started if copy is not used[message]]
        encode(total, rs_out, at, rows)
        where = {"space": space_at(hop)} if kind == "space" else {"slot": slot_at(hop)}
        sums[i, message] = used[message] = send(rs_out.at[at], rs_in.at[at], rs_s.at[i, at], rs_r.at[i, at], where)

    def height(message):
        return 1 + max([height(child) for child in children.get(message, [])], default=0)

    def gather_terms(i):
        order = sorted(range(chips), key=lambda k: (-min(k, chips - k), k))
        left = list(hops)
        for k in order:
            force(i, k)
            for message in [v for v in left if v[1] == k and v not in children]:
                pass_up(i, message)
                left.remove(message)
        for message in sorted(left, key=lambda v: (height(v), -distance(v, chips))):
            pass_up(i, message)
        for j in range(per):
            at = slice(j * BLOCK, (j + 1) * BLOCK)
            if i:
                second_ref[:, at] = step[:, at] + partial(i, (0, 0, j))
            else:
                base = control[:, at].astype(F32)
                total = base + partial(i, (0, 0, j))
                first_ref[:, at] = total
                moved_on = base - descent_step * total
                step[:, at] = moved_on
                encode(moved_on, coded[0], per * me + j, rows)
                pass_on(1, (0, 0, j))

    deepest = max(distance(v, chips) for v in hops)
    reach = spaces.bit_length() - 1

    quarters = list(range(nobs // OBS_CHUNK))
    for depth in range(1, deepest + 1):
        relay(0, depth)
        if quarters:
            build_pick(quarters.pop(0))
    for q in quarters:
        build_pick(q)
    for arrive in moved:
        arrive()
    for k in range(chips):
        spread(0, k, k == 0)
    observe_all(0)
    gather_terms(0)
    done = []
    for depth in range(1, deepest + 1):
        relay(1, depth)
        for k in range(chips):
            if min(k, chips - k) + reach == depth:
                spread(1, k, not done)
                done.append(k)
    observe_all(1)
    gather_terms(1)
    for copy in started:
        copy.wait_send()


def per_device(control, block_lists, loc_tiles, ensemble, obs_col, obs_wts, innovation, inv_error):
    rows, width = control.shape
    cells = ensemble.shape[2]
    nobs = obs_col.shape[1]
    spaces, slots = lax.axis_size("space"), lax.axis_size("slot")
    chips = slots // CORES
    per = width // BLOCK
    ncb = spaces * per
    blocks = cells // BLOCK
    messages = per * spaces * chips
    dma = pltpu.SemaphoreType.DMA
    vmem = pl.BlockSpec(memory_space=pltpu.VMEM)
    out = jax.ShapeDtypeStruct((rows, width), F32)
    return pl.pallas_call(
        functools.partial(kernel, spaces, slots),
        out_shape=(out, out),
        in_specs=[
            vmem, pl.BlockSpec(memory_space=pltpu.SMEM), vmem, pl.BlockSpec(memory_space=pl.ANY),
            vmem, vmem, vmem, vmem,
        ],
        out_specs=(vmem, vmem),
        scratch_shapes=[pltpu.VMEM((ncb, rows, BLOCK), BF16)] * chips
        + [pltpu.VMEM((ncb, rows + PAD, BLOCK), I16)] * chips
        + [
            pltpu.VMEM((CORES, chips, rows, cells), BF16),
            pltpu.VMEM((blocks, 2 * BLOCK, BLOCK), BF16),
            pltpu.VMEM((ncb, 2 * BLOCK, BLOCK), BF16),
            pltpu.SMEM((ncb, 2), I32),
            pltpu.VMEM((nobs // OBS_CHUNK, cells, OBS_CHUNK), BF16),
            pltpu.VMEM((nobs // OBS_CHUNK, OBS_CHUNK, cells), BF16),
            pltpu.VMEM((LEV, cells), F32),
            pltpu.VMEM((2, LEV, cells), F32),
            pltpu.VMEM((2, LEV, cells), F32),
            pltpu.VMEM((2 * LEV, cells), BF16),
            pltpu.VMEM((2, LEV, cells), F32),
            pltpu.VMEM((2, LEV, cells), F32),
            pltpu.VMEM((ncb, 2 * rows, BLOCK), BF16),
            pltpu.VMEM((blocks, 2 * rows, BLOCK), BF16),
            pltpu.VMEM((chips, ncb, rows, BLOCK), F32),
            pltpu.VMEM((rows, width), F32),
            pltpu.VMEM((messages, rows + PAD, BLOCK), I16),
            pltpu.VMEM((messages, rows + PAD, BLOCK), I16),
            dma((chips,)), dma((chips,)), dma((chips,)),
            dma((2, messages)), dma((2, messages)),
            dma((2, messages)), dma((2, messages)),
            dma((2, 2)), dma((2, 2)),
        ],
        compiler_params=pltpu.CompilerParams(
            collective_id=0, has_side_effects=True, vmem_limit_bytes=58 * 1024 * 1024
        ),
        name="envar_gradients",
    )(
        control, block_lists, loc_tiles, ensemble.reshape(slots, rows, cells), obs_col,
        obs_wts, innovation, inv_error,
    )


def solution(mesh):
    placed = (
        P("slot", "space"),
        P("space", None),
        P("space", None, None, None),
        P("slot", None, "space"),
        P("slot", "space"),
        P("slot", None, "space"),
        P("slot", "space"),
        P("slot", "space"),
    )
    return jax.shard_map(
        per_device,
        mesh=mesh,
        in_specs=placed,
        out_specs=(P("slot", "space"), P("slot", "space")),
        check_vma=False,
    )
```

```python
import functools

import jax
import jax.numpy as jnp
from jax import lax
from jax.experimental import pallas as pl
from jax.experimental.pallas import tpu as pltpu
from jax.sharding import PartitionSpec as P

LEV = 48
BLOCK = 128
CORES = 2
OBS_CHUNK = 512
PAD = 16
TOP = 32700.0
FINE = 256.0
descent_step = 0.5
F32 = jnp.float32
BF16 = jnp.bfloat16
I16 = jnp.int16
I32 = jnp.int32
MESH = pl.DeviceIdType.MESH


def halves(x):
    high = x.astype(BF16)
    return high, (x - high.astype(F32)).astype(BF16)


def dot(a, b):
    return lax.dot_general(a, b, (((1,), (0,)), ((), ())), preferred_element_type=F32)


HOP, EXTRA, FLIT = 2.1, 0.5, 1.1
FORCE, MIX, CODE, UNCODE, ROOT, RELAY, FIRST, SECOND, TABLE = 0.9, 0.4, 0.1, 0.03, 0.25, 0.03, 1.3, 1.9, 0.4


def bits_of(m):
    return [1 << i for i in range(m.bit_length()) if m >> i & 1]


def tree(spaces, chips, per):
    hops, children = {}, {}
    for j in range(per):
        for m in range(spaces):
            for k in range(chips):
                if m:
                    bits = bits_of(m)
                    hop = (bits[(len(bits_of(k)) + j) % len(bits)], 0)
                elif k:
                    hop = (0, k)
                else:
                    continue
                hops[m, k, j] = hop
                children.setdefault((m ^ hop[0], k ^ hop[1], j), []).append((m, k, j))
    return hops, children


def arrival(hop, at, links):
    flips, k = hop
    if flips:
        uses = [(("space", flips), FLIT)]
    else:
        uses = [("end", FLIT)] if k == 1 else [("middle", 2 * FLIT)]
    for link, takes in uses:
        at = max(at, links.get(link, 0.0)) + takes
        links[link] = at
    return at + HOP + EXTRA * (k > 1)


def ordered(tasks):
    sender = {v: name for name, (_, _, _, sends) in tasks.items() for v, _ in sends}
    hop_of = {v: hop for _, _, _, sends in tasks.values() for v, hop in sends}
    after = {name: [] for name in tasks}
    for name, (_, ends, takes, _) in tasks.items():
        for other in ends:
            after[other].append((name, 0.0))
        for v in takes:
            after[sender[v]].append((name, HOP + FLIT * (1 + (hop_of[v][1] > 1))))
    rest = {}

    def remaining(name):
        if name not in rest:
            rest[name] = tasks[name][0] + max([gap + remaining(v) for v, gap in after[name]], default=0.0)
        return rest[name]

    now, links, ended, there, order = 0.0, {}, {}, {}, []
    left = list(tasks)
    while left:
        ready = {}
        for name in left:
            _, ends, takes, _ = tasks[name]
            if all(v in ended for v in ends) and all(v in there for v in takes):
                ready[name] = max([ended[v] for v in ends] + [there[v] for v in takes], default=0.0)
        able = [v for v in ready if ready[v] <= now]
        if not able:
            now = min(ready.values())
            able = [v for v in ready if ready[v] <= now]
        name = max(able, key=remaining)
        takes_time, _, _, sends = tasks[name]
        now += takes_time
        ended[name] = now
        for v, hop in sends:
            there[v] = arrival(hop, now, links)
        order.append(name)
        left.remove(name)
    return order


def encode(x, ref, slot, rows):
    top = jnp.max(jnp.abs(x), axis=0, keepdims=True)
    log = jnp.ceil(jnp.log2(jnp.maximum(top, 1e-36)) * FINE)
    log = jnp.clip(log, -126.0 * FINE, 126.0 * FINE)
    scale = jnp.exp2(log * (1.0 / FINE)) * (1.0 / TOP)
    ref[slot, :rows] = jnp.round(x * (1.0 / scale)).astype(I32).astype(I16)
    ref[slot, rows : rows + PAD] = jnp.broadcast_to(log, (PAD, BLOCK)).astype(I32).astype(I16)


def decode(ref, slot, rows):
    log = ref[slot, rows : rows + PAD].astype(I32).astype(F32)[:1]
    scale = jnp.exp2(log * (1.0 / FINE)) * (1.0 / TOP)
    return ref[slot, :rows].astype(I32).astype(F32) * scale


def kernel(spaces, slots, *refs):
    chips = slots // CORES
    (control, lists, tiles, ensemble, cols, wts, innovation, inverse, first_ref, second_ref) = refs[:10]
    ctl, coded = refs[10 : 10 + chips], refs[10 + chips : 10 + 2 * chips]
    (
        ens, tiles_t, tiles_a, inv, pick, pick_t, inc, inc_out, inc_in, pair, adj, adj_in, split, forced, con,
        rs_out, rs_in, own_s, ens_s, ens_r, ag_s, ag_r, rs_s, rs_r, x_s, x_r,
    ) = refs[10 + 2 * chips :]
    rows, width = control.shape
    per = width // BLOCK
    cells = ensemble.shape[2]
    nobs = cols.shape[1]
    blocks = cells // BLOCK
    listed = lists.shape[0]
    ncb = spaces * per
    members = rows // LEV
    me = lax.axis_index("space")
    slot = lax.axis_index("slot")
    z, core = slot // CORES, lax.rem(slot, CORES)
    sibling = {"slot": slot + 1 - 2 * core}
    hops, children = tree(spaces, chips, per)

    def flipped(index, flips):
        at = index
        for bit in bits_of(flips):
            at = at + bit * (1 - 2 * lax.rem(index // bit, 2))
        return at

    def space_at(m):
        return flipped(me, m)

    def device_at(hop):
        where = {}
        if hop[0]:
            where["space"] = flipped(me, hop[0])
        if hop[1]:
            where["slot"] = flipped(z, hop[1]) * CORES + core
        return where

    def number(message):
        m, k, j = message
        return (j * spaces + m) * chips + k

    barrier = pltpu.get_barrier_semaphore()
    near = [device_at(hop) for hop in sorted(set(hops.values()))] + [sibling]
    for where in near:
        pl.semaphore_signal(barrier, inc=1, device_id=where, device_id_type=MESH)
    pl.semaphore_wait(barrier, len(near))

    started = []

    def send(src, dst, ssem, rsem, where):
        copy = pltpu.make_async_remote_copy(
            src_ref=src, dst_ref=dst, send_sem=ssem, recv_sem=rsem,
            device_id=where, device_id_type=MESH,
        )
        copy.start()
        started.append(copy)
        return copy

    gathers = {}

    def pass_on(i, message):
        m, k, j = message
        held = coded if i else ctl
        at = per * space_at(m) + j
        for child in children.get(message, []):
            to = number(child)
            gathers[i, child] = send(
                held[k].at[at], held[child[1]].at[at], ag_s.at[i, to], ag_r.at[i, to], device_at(hops[child])
            )

    def relay(i, message):
        gathers[i, message].wait_recv()
        pass_on(i, message)

    for j in range(per):
        ctl[0][per * me + j] = control[:, j * BLOCK : (j + 1) * BLOCK]
    for j in range(per):
        pass_on(0, (0, 0, j))
    moved = {}
    for k in range(chips):
        there = flipped(z, k) * CORES
        moved[k] = [send(ensemble.at[there + 1 - core], ens.at[1, k], ens_s.at[k], ens_r.at[k], sibling).wait_recv]
        own = pltpu.make_async_copy(ensemble.at[there + core], ens.at[0, k], own_s.at[k])
        own.start()
        moved[k].append(own.wait)

    def build_tiles(g, carry):
        for e in range(listed):
            tiles_t[g, e * BLOCK : (e + 1) * BLOCK] = tiles[g, e].astype(F32).T.astype(BF16)
        return carry

    def build_adjoint(b, carry):
        one, two = jnp.int32(-1), jnp.int32(-1)
        for g in range(blocks):
            for e in range(listed):
                hit = lists[e, g] == b
                two = jnp.where(hit, jnp.where(one >= 0, g * listed + e, two), two)
                one = jnp.where(hit, jnp.where(one >= 0, one, g * listed + e), one)
        for place, found in enumerate((one, two)):
            kept = jnp.where(found >= 0, 1.0, 0.0)
            found = jnp.maximum(found, 0)
            g = found // listed
            inv[b, place] = g
            tile = tiles[g, lax.rem(found, listed)].astype(F32) * kept
            tiles_a[b, place * BLOCK : (place + 1) * BLOCK] = tile.astype(BF16)
        return carry

    first_cell = me * cells

    def build_pick(q):
        line = cols[:, q * OBS_CHUNK : (q + 1) * OBS_CHUNK] - first_cell

        def band(r, carry):
            rowid = lax.broadcasted_iota(I32, (BLOCK, OBS_CHUNK), 0) + r * BLOCK
            at = pl.ds(pl.multiple_of(r * BLOCK, BLOCK), BLOCK)
            pick[q, at] = jnp.where(rowid == line, 1.0, 0.0).astype(BF16)
            return carry

        lax.fori_loop(0, blocks, band, 0)
        turned = [
            jnp.broadcast_to(line[:, h * BLOCK : (h + 1) * BLOCK].astype(F32), (BLOCK, BLOCK)).T
            for h in range(OBS_CHUNK // BLOCK)
        ]

        def band_t(r, carry):
            lane = (lax.broadcasted_iota(I32, (BLOCK, BLOCK), 1) + r * BLOCK).astype(F32)
            at = pl.ds(pl.multiple_of(r * BLOCK, BLOCK), BLOCK)
            for h, column in enumerate(turned):
                pick_t[q, h * BLOCK : (h + 1) * BLOCK, at] = jnp.where(column == lane, 1.0, 0.0).astype(BF16)
            return carry

        lax.fori_loop(0, blocks, band_t, 0)

    def tables_of_tiles():
        lax.fori_loop(0, blocks, build_tiles, 0)

    def tables_of_adjoint():
        lax.fori_loop(0, ncb, build_adjoint, 0)

    def member(n):
        return slice(n * LEV, (n + 1) * LEV)

    def lanes(g):
        return pl.ds(pl.multiple_of(g * BLOCK, BLOCK), BLOCK)

    spread_yet = set()

    def spread(i, k):
        fresh = i not in spread_yet
        spread_yet.add(i)
        for m in range(spaces):
            for j in range(per):
                if (m or k) and (m, k, j) not in children:
                    gathers[i, (m, k, j)].wait_recv()
        if not i:
            for arrive in moved[k]:
                arrive()
        if i:

            def unpack(b, carry):
                up, down = halves(decode(coded[k], b, rows))
                split[b, :rows] = up
                split[b, rows:] = down
                return carry

            lax.fori_loop(0, ncb, unpack, 0, unroll=4)

        def run(g, carry):
            held = split if i else ctl[k]
            left = jnp.concatenate([held[lists[e, g]] for e in range(listed)], axis=1)
            value = dot(left, tiles_t[g])
            if i:
                value = value[:rows] + value[rows:]
            at = lanes(g)
            for s, target in enumerate((inc, inc_out.at[i])):
                total = None if fresh else target[:, at]
                for n in range(members):
                    term = ens[s, k, member(n), at].astype(F32) * value[member(n)]
                    total = term if total is None else total + term
                target[:, at] = total
            return carry

        lax.fori_loop(0, blocks, run, 0, unroll=4)

    def observe_all(i):
        swap = send(inc_out.at[i], inc_in.at[i], x_s.at[i, 0], x_r.at[i, 0], sibling)
        swap.wait_recv()
        high, low = halves(inc[...] + inc_in[i])
        pair[:LEV] = high
        pair[LEV:] = low
        adj[i] = jnp.zeros((LEV, cells), F32)

        def observe(q, carry):
            at = pl.ds(pl.multiple_of(q * OBS_CHUNK, OBS_CHUNK), OBS_CHUNK)
            seen = dot(pair[...], pick[q])
            seen = seen[:LEV] + seen[LEV:]
            w = wts[0, :, at]
            modelled = jnp.sum(w * seen, axis=0, keepdims=True)
            residual = inverse[:, at] * (modelled - innovation[:, at])
            up, down = halves(w * residual)
            back = dot(jnp.concatenate([up, down], axis=0), pick_t[q])
            adj[i] += back[:LEV] + back[LEV:]
            return carry

        lax.fori_loop(0, nobs // OBS_CHUNK, observe, 0)
        swap = send(adj.at[i], adj_in.at[i], x_s.at[i, 1], x_r.at[i, 1], sibling)
        swap.wait_recv()

    def force(i, k):
        def fill(g, carry):
            at = lanes(g)
            mine, other = adj[i, :, at], adj_in[i, :, at]
            for n in range(members):
                total = ens[0, k, member(n), at].astype(F32) * mine + ens[1, k, member(n), at].astype(F32) * other
                up, down = halves(total)
                forced[g, member(n)] = up
                forced[g, rows + n * LEV : rows + (n + 1) * LEV] = down
            return carry

        lax.fori_loop(0, blocks, fill, 0, unroll=4)

    def mix(k, j):
        def multiply(q, carry):
            b = per * q + j
            left = jnp.concatenate([forced[inv[b, place]] for place in range(2)], axis=1)
            both = dot(left, tiles_a[b])
            con[k, b] = both[:rows] + both[rows:]
            return carry

        lax.fori_loop(0, spaces, multiply, 0, unroll=4)

    sums, used = {}, {}

    def partial(i, message):
        m, k, j = message
        total = con[k, per * space_at(m) + j]
        for child in children.get(message, []):
            sums[i, child].wait_recv()
            total = total + decode(rs_in, number(child), rows)
        return total

    def pass_up(i, message):
        at = number(message)
        total = partial(i, message)
        if message in used:
            used[message].wait_send()
            started[:] = [copy for copy in started if copy is not used[message]]
        encode(total, rs_out, at, rows)
        sums[i, message] = used[message] = send(
            rs_out.at[at], rs_in.at[at], rs_s.at[i, at], rs_r.at[i, at], device_at(hops[message])
        )

    def root(i, j):
        at = slice(j * BLOCK, (j + 1) * BLOCK)
        base = control[:, at].astype(F32)
        terms = partial(i, (0, 0, j))
        if i:
            second_ref[:, at] = terms
        else:
            first_ref[:, at] = terms
            moved_on = base - descent_step * (base + terms)
            encode(moved_on, coded[0], per * me + j, rows)
            pass_on(1, (0, 0, j))

    far_first = sorted(range(chips), key=lambda k: (-k, k))
    near_first = sorted(range(chips))

    def gathering(i, tasks, roots):
        names = {}
        for message in hops:
            if message in children:
                sends = [((i, child), hops[child]) for child in children[message]]
                tasks[relay, i, message] = (RELAY, [], [(i, message)], sends)
        for k in near_first:
            needs = [(relay, i, (m, k, j)) for m in range(spaces) for j in range(per) if (m, k, j) in children and (m or k)]
            takes = [(i, (m, k, j)) for m in range(spaces) for j in range(per) if (m, k, j) not in children]
            tasks[spread, i, k] = (SECOND if i else FIRST, needs + roots, takes, [])

    def summing(i, tasks):
        before = []
        for k in far_first:
            tasks[force, i, k] = (FORCE, before, [], [])
            before = []
            for j in range(per):
                tasks[mix, k, j] = (MIX, [(force, i, k)], [], [])
                before.append((mix, k, j))
        for message, hop in hops.items():
            takes = [(i, "sum", child) for child in children.get(message, [])]
            tasks[pass_up, i, message] = (
                CODE + UNCODE * len(takes), [(mix, *message[1:])], takes, [((i, "sum", message), hop)]
            )
        for j in range(per):
            takes = [(i, "sum", child) for child in children[0, 0, j]]
            sends = [] if i else [((1, child), hops[child]) for child in children[0, 0, j]]
            tasks[root, i, j] = (ROOT, [(mix, 0, j)], takes, sends)

    def run(tasks):
        for name in ordered(tasks):
            name[0](*name[1:])

    tables = [(tables_of_tiles,), (tables_of_adjoint,)] + [(build_pick, q) for q in range(nobs // OBS_CHUNK)]
    tasks = {}
    tasks["start",] = (0.0, [], [], [((0, child), hops[child]) for j in range(per) for child in children[0, 0, j]])
    for name in tables:
        tasks[name] = (TABLE, [], [], [])
    gathering(0, tasks, [(tables_of_tiles,)])
    for name in ordered(tasks):
        if name != ("start",):
            name[0](*name[1:])
    observe_all(0)
    tasks = {}
    summing(0, tasks)
    gathering(1, tasks, [(root, 0, j) for j in range(per)])
    run(tasks)
    observe_all(1)
    tasks = {}
    summing(1, tasks)
    run(tasks)
    for copy in started:
        copy.wait_send()


def per_device(control, block_lists, loc_tiles, ensemble, obs_col, obs_wts, innovation, inv_error):
    rows, width = control.shape
    cells = ensemble.shape[2]
    nobs = obs_col.shape[1]
    spaces, slots = lax.axis_size("space"), lax.axis_size("slot")
    chips = slots // CORES
    per = width // BLOCK
    ncb = spaces * per
    blocks = cells // BLOCK
    messages = per * spaces * chips
    dma = pltpu.SemaphoreType.DMA
    vmem = pl.BlockSpec(memory_space=pltpu.VMEM)
    out = jax.ShapeDtypeStruct((rows, width), F32)
    first, second = pl.pallas_call(
        functools.partial(kernel, spaces, slots),
        out_shape=(out, out),
        in_specs=[
            vmem, pl.BlockSpec(memory_space=pltpu.SMEM), vmem, pl.BlockSpec(memory_space=pl.ANY),
            vmem, vmem, vmem, vmem,
        ],
        out_specs=(vmem, vmem),
        scratch_shapes=[pltpu.VMEM((ncb, rows, BLOCK), BF16)] * chips
        + [pltpu.VMEM((ncb, rows + PAD, BLOCK), I16)] * chips
        + [
            pltpu.VMEM((CORES, chips, rows, cells), BF16),
            pltpu.VMEM((blocks, 2 * BLOCK, BLOCK), BF16),
            pltpu.VMEM((ncb, 2 * BLOCK, BLOCK), BF16),
            pltpu.SMEM((ncb, 2), I32),
            pltpu.VMEM((nobs // OBS_CHUNK, cells, OBS_CHUNK), BF16),
            pltpu.VMEM((nobs // OBS_CHUNK, OBS_CHUNK, cells), BF16),
            pltpu.VMEM((LEV, cells), F32),
            pltpu.VMEM((2, LEV, cells), F32),
            pltpu.VMEM((2, LEV, cells), F32),
            pltpu.VMEM((2 * LEV, cells), BF16),
            pltpu.VMEM((2, LEV, cells), F32),
            pltpu.VMEM((2, LEV, cells), F32),
            pltpu.VMEM((ncb, 2 * rows, BLOCK), BF16),
            pltpu.VMEM((blocks, 2 * rows, BLOCK), BF16),
            pltpu.VMEM((chips, ncb, rows, BLOCK), F32),
            pltpu.VMEM((messages, rows + PAD, BLOCK), I16),
            pltpu.VMEM((messages, rows + PAD, BLOCK), I16),
            dma((chips,)), dma((chips,)), dma((chips,)),
            dma((2, messages)), dma((2, messages)),
            dma((2, messages)), dma((2, messages)),
            dma((2, 2)), dma((2, 2)),
        ],
        compiler_params=pltpu.CompilerParams(
            collective_id=0, has_side_effects=True, vmem_limit_bytes=58 * 1024 * 1024
        ),
        name="envar_gradients",
    )(
        control, block_lists.T, loc_tiles, ensemble.reshape(slots, rows, cells), obs_col,
        obs_wts, innovation, inv_error,
    )
    base = control.astype(F32)
    first = base + first
    return first, (base - descent_step * first) + second


def solution(mesh):
    placed = (
        P("slot", "space"),
        P("space", None),
        P("space", None, None, None),
        P("slot", None, "space"),
        P("slot", "space"),
        P("slot", None, "space"),
        P("slot", "space"),
        P("slot", "space"),
    )
    return jax.shard_map(
        per_device,
        mesh=mesh,
        in_specs=placed,
        out_specs=(P("slot", "space"), P("slot", "space")),
        check_vma=False,
    )
```

```python
import functools

import jax
import jax.numpy as jnp
from jax import lax
from jax.experimental import pallas as pl
from jax.experimental.pallas import tpu as pltpu
from jax.sharding import PartitionSpec as P

LEV = 48
BLOCK = 128
CORES = 2
OBS_CHUNK = 512
PAD = 16
TOP = 32700.0
FINE = 256.0
descent_step = 0.5
F32 = jnp.float32
BF16 = jnp.bfloat16
I16 = jnp.int16
I32 = jnp.int32
MESH = pl.DeviceIdType.MESH


def halves(x):
    high = x.astype(BF16)
    return high, (x - high.astype(F32)).astype(BF16)


def dot(a, b):
    return lax.dot_general(a, b, (((1,), (0,)), ((), ())), preferred_element_type=F32)


HOP, EXTRA, FLIT = 2.1, 0.5, 1.1
FORCE, MIX, CODE, UNCODE, ROOT, RELAY, FIRST, SECOND, TABLE = 0.45, 0.15, 0.08, 0.03, 0.2, 0.03, 0.7, 1.0, 0.4


def bits_of(m):
    return [1 << i for i in range(m.bit_length()) if m >> i & 1]


PIECES = 1
TREE = ((0, 0, 0, 2, 0, 1, 2, 3, 0, 1, 2, 3, 4, 5, 6, 12), (0, 2, 0, 2, 0, 4, 2, 3, 0, 8, 2, 8, 8, 9, 6, 11))


def tree(spaces, chips, per):
    hops, children = {}, {}
    for j in range(per):
        for m in range(spaces):
            for k in range(chips):
                bits = bits_of(m)
                if TREE and (spaces, chips, per) == (4, 4, len(TREE)):
                    above = TREE[j][m * chips + k]
                    hop = (m ^ above // chips, k ^ above % chips)
                    if not any(hop):
                        continue
                elif k % 2 and (j % 2 or not m):
                    hop = (0, 1)
                elif m:
                    hop = (bits[(len(bits_of(k)) + j) % len(bits)], 0)
                elif k:
                    hop = (0, k)
                else:
                    continue
                hops[m, k, j] = hop
                children.setdefault((m ^ hop[0], k ^ hop[1], j), []).append((m, k, j))
    below = {}

    def height(message):
        if message not in below:
            below[message] = 1 + max([height(child) for child in children.get(message, [])], default=0)
        return below[message]

    for group in children.values():
        group.sort(key=height, reverse=True)
    return hops, children


def arrival(hop, at, links):
    flips, k = hop
    if flips:
        uses = [(("space", flips), FLIT)]
    else:
        uses = [("end", FLIT)] if k == 1 else [("end", FLIT), ("middle", 2 * FLIT)]
    for link, takes in uses:
        at = max(at, links.get(link, 0.0)) + takes
        links[link] = at
    return at + HOP + EXTRA * (k > 1)


def ordered(tasks):
    sender = {v: name for name, (_, _, _, sends) in tasks.items() for v, _ in sends}
    hop_of = {v: hop for _, _, _, sends in tasks.values() for v, hop in sends}
    after = {name: [] for name in tasks}
    for name, (_, ends, takes, _) in tasks.items():
        for other in ends:
            after[other].append((name, 0.0))
        for v in takes:
            after[sender[v]].append((name, HOP + FLIT * (1 + (hop_of[v][1] > 1))))
    rest = {}

    def remaining(name):
        if name not in rest:
            rest[name] = tasks[name][0] + max([gap + remaining(v) for v, gap in after[name]], default=0.0)
        return rest[name]

    now, links, ended, there, order = 0.0, {}, {}, {}, []
    left = list(tasks)
    while left:
        ready = {}
        for name in left:
            _, ends, takes, _ = tasks[name]
            if all(v in ended for v in ends) and all(v in there for v in takes):
                ready[name] = max([ended[v] for v in ends] + [there[v] for v in takes], default=0.0)
        able = [v for v in ready if ready[v] <= now]
        if not able:
            now = min(ready.values())
            able = [v for v in ready if ready[v] <= now]
        name = max(able, key=remaining)
        takes_time, _, _, sends = tasks[name]
        now += takes_time
        ended[name] = now
        for v, hop in sends:
            there[v] = arrival(hop, now, links)
        order.append(name)
        left.remove(name)
    return order


def encode(x, ref):
    rows = x.shape[0]
    top = jnp.max(jnp.abs(x), axis=0, keepdims=True)
    log = jnp.ceil(jnp.log2(jnp.maximum(top, 1e-36)) * FINE)
    log = jnp.clip(log, -126.0 * FINE, 126.0 * FINE)
    scale = jnp.exp2(log * (1.0 / FINE)) * (1.0 / TOP)
    ref[:rows] = jnp.round(x * (1.0 / scale)).astype(I32).astype(I16)
    ref[rows : rows + PAD] = jnp.broadcast_to(log, (PAD, BLOCK)).astype(I32).astype(I16)


def decode(ref):
    rows = ref.shape[0] - PAD
    log = ref[rows : rows + PAD].astype(I32).astype(F32)[:1]
    scale = jnp.exp2(log * (1.0 / FINE)) * (1.0 / TOP)
    return ref[:rows].astype(I32).astype(F32) * scale


def kernel(spaces, slots, *refs):
    chips = slots // CORES
    (control, lists, tiles, ensemble, cols, wts, innovation, inverse, first_ref, second_ref) = refs[:10]
    ctl, coded = refs[10 : 10 + chips], refs[10 + chips : 10 + 2 * chips]
    (
        ens, tiles_t, tiles_a, inv, pick, pick_t, inc, inc_out, inc_in, pair, adj, adj_in, split, forced, con,
        rs_out, rs_in, own_s, ens_s, ens_r, ag_s, ag_r, rs_s, rs_r, x_s, x_r,
    ) = refs[10 + 2 * chips :]
    rows, width = control.shape
    per = width // BLOCK
    cells = ensemble.shape[2]
    nobs = cols.shape[1]
    blocks = cells // BLOCK
    listed = lists.shape[0]
    ncb = spaces * per
    members = rows // LEV
    me = lax.axis_index("space")
    slot = lax.axis_index("slot")
    z, core = slot // CORES, lax.rem(slot, CORES)
    sibling = {"slot": slot + 1 - 2 * core}
    part = rows // PIECES
    hops, children = tree(spaces, chips, per * PIECES)

    def flipped(index, flips):
        at = index
        for bit in bits_of(flips):
            at = at + bit * (1 - 2 * lax.rem(index // bit, 2))
        return at

    def space_at(m):
        return flipped(me, m)

    def device_at(hop):
        where = {}
        if hop[0]:
            where["space"] = flipped(me, hop[0])
        if hop[1]:
            where["slot"] = flipped(z, hop[1]) * CORES + core
        return where

    def number(message):
        m, k, j = message
        return (j * spaces + m) * chips + k

    barrier = pltpu.get_barrier_semaphore()
    near = [device_at(hop) for hop in sorted(set(hops.values()))] + [sibling]
    for where in near:
        pl.semaphore_signal(barrier, inc=1, device_id=where, device_id_type=MESH)
    pl.semaphore_wait(barrier, len(near))

    started = []

    def send(src, dst, ssem, rsem, where):
        copy = pltpu.make_async_remote_copy(
            src_ref=src, dst_ref=dst, send_sem=ssem, recv_sem=rsem,
            device_id=where, device_id_type=MESH,
        )
        copy.start()
        started.append(copy)
        return copy

    gathers = {}

    def kept(i, k, m, j):
        at, r = per * space_at(m) + j % per, j // per
        if i:
            return coded[k].at[at, pl.ds(r * (part + PAD), part + PAD)]
        return ctl[k].at[at, pl.ds(r * part, part)]

    def pass_on(i, message):
        m, k, j = message
        for child in children.get(message, []):
            to = number(child)
            gathers[i, child] = send(
                kept(i, k, m, j), kept(i, child[1], m, j), ag_s.at[i, to], ag_r.at[i, to], device_at(hops[child])
            )

    def relay(i, message):
        gathers[i, message].wait_recv()
        pass_on(i, message)

    for j in range(per):
        ctl[0][per * me + j] = control[:, j * BLOCK : (j + 1) * BLOCK]
    for j in range(per * PIECES):
        pass_on(0, (0, 0, j))
    moved = {}
    for k in range(chips):
        there = flipped(z, k) * CORES
        moved[k] = [send(ensemble.at[there + 1 - core], ens.at[1, k], ens_s.at[k], ens_r.at[k], sibling).wait_recv]
        own = pltpu.make_async_copy(ensemble.at[there + core], ens.at[0, k], own_s.at[k])
        own.start()
        moved[k].append(own.wait)

    def build_tiles(g, carry):
        for e in range(listed):
            tiles_t[g, e * BLOCK : (e + 1) * BLOCK] = tiles[g, e].astype(F32).T.astype(BF16)
        return carry

    def build_adjoint(b, carry):
        one, two = jnp.int32(-1), jnp.int32(-1)
        for g in range(blocks):
            for e in range(listed):
                hit = lists[e, g] == b
                two = jnp.where(hit, jnp.where(one >= 0, g * listed + e, two), two)
                one = jnp.where(hit, jnp.where(one >= 0, one, g * listed + e), one)
        for place, found in enumerate((one, two)):
            kept = jnp.where(found >= 0, 1.0, 0.0)
            found = jnp.maximum(found, 0)
            g = found // listed
            inv[b, place] = g
            tile = tiles[g, lax.rem(found, listed)].astype(F32) * kept
            tiles_a[b, place * BLOCK : (place + 1) * BLOCK] = tile.astype(BF16)
        return carry

    first_cell = me * cells

    def build_pick(q):
        line = cols[:, q * OBS_CHUNK : (q + 1) * OBS_CHUNK] - first_cell

        def band(r, carry):
            rowid = lax.broadcasted_iota(I32, (BLOCK, OBS_CHUNK), 0) + r * BLOCK
            at = pl.ds(pl.multiple_of(r * BLOCK, BLOCK), BLOCK)
            pick[q, at] = jnp.where(rowid == line, 1.0, 0.0).astype(BF16)
            return carry

        lax.fori_loop(0, blocks, band, 0)
        turned = [
            jnp.broadcast_to(line[:, h * BLOCK : (h + 1) * BLOCK].astype(F32), (BLOCK, BLOCK)).T
            for h in range(OBS_CHUNK // BLOCK)
        ]

        def band_t(r, carry):
            lane = (lax.broadcasted_iota(I32, (BLOCK, BLOCK), 1) + r * BLOCK).astype(F32)
            at = pl.ds(pl.multiple_of(r * BLOCK, BLOCK), BLOCK)
            for h, column in enumerate(turned):
                pick_t[q, h * BLOCK : (h + 1) * BLOCK, at] = jnp.where(column == lane, 1.0, 0.0).astype(BF16)
            return carry

        lax.fori_loop(0, blocks, band_t, 0)

    def tables_of_tiles():
        lax.fori_loop(0, blocks, build_tiles, 0)

    def tables_of_adjoint():
        lax.fori_loop(0, ncb, build_adjoint, 0)

    def member(n):
        return slice(n * LEV, (n + 1) * LEV)

    def lanes(g):
        return pl.ds(pl.multiple_of(g * BLOCK, BLOCK), BLOCK)

    spread_yet = set()

    def spread(i, k):
        fresh = i not in spread_yet
        spread_yet.add(i)
        for m in range(spaces):
            for j in range(per * PIECES):
                if (m or k) and (m, k, j) not in children:
                    gathers[i, (m, k, j)].wait_recv()
        if not i:
            for arrive in moved[k]:
                arrive()
        if i:

            def unpack(b, carry):
                for r in range(PIECES):
                    at = r * (part + PAD)
                    up, down = halves(decode(coded[k].at[b, at : at + part + PAD]))
                    split[b, r * part : (r + 1) * part] = up
                    split[b, rows + r * part : rows + (r + 1) * part] = down
                return carry

            lax.fori_loop(0, ncb, unpack, 0, unroll=2)

        def run(g, carry):
            held = split if i else ctl[k]
            left = jnp.concatenate([held[lists[e, g]] for e in range(listed)], axis=1)
            value = dot(left, tiles_t[g])
            if i:
                value = value[:rows] + value[rows:]
            at = lanes(g)
            for s, target in enumerate((inc, inc_out.at[i])):
                total = None if fresh else target[:, at]
                for n in range(members):
                    term = ens[s, k, member(n), at].astype(F32) * value[member(n)]
                    total = term if total is None else total + term
                target[:, at] = total
            return carry

        lax.fori_loop(0, blocks, run, 0, unroll=4)

    def observe_all(i):
        swap = send(inc_out.at[i], inc_in.at[i], x_s.at[i, 0], x_r.at[i, 0], sibling)
        swap.wait_recv()
        high, low = halves(inc[...] + inc_in[i])
        pair[:LEV] = high
        pair[LEV:] = low
        adj[i] = jnp.zeros((LEV, cells), F32)

        def observe(q, carry):
            at = pl.ds(pl.multiple_of(q * OBS_CHUNK, OBS_CHUNK), OBS_CHUNK)
            seen = dot(pair[...], pick[q])
            seen = seen[:LEV] + seen[LEV:]
            w = wts[0, :, at]
            modelled = jnp.sum(w * seen, axis=0, keepdims=True)
            residual = inverse[:, at] * (modelled - innovation[:, at])
            up, down = halves(w * residual)
            back = dot(jnp.concatenate([up, down], axis=0), pick_t[q])
            adj[i] += back[:LEV] + back[LEV:]
            return carry

        lax.fori_loop(0, nobs // OBS_CHUNK, observe, 0, unroll=True)
        swap = send(adj.at[i], adj_in.at[i], x_s.at[i, 1], x_r.at[i, 1], sibling)
        swap.wait_recv()

    def force(i, k):
        def fill(g, carry):
            at = lanes(g)
            mine, other = adj[i, :, at], adj_in[i, :, at]
            for n in range(members):
                total = ens[0, k, member(n), at].astype(F32) * mine + ens[1, k, member(n), at].astype(F32) * other
                up, down = halves(total)
                forced[g, member(n)] = up
                forced[g, rows + n * LEV : rows + (n + 1) * LEV] = down
            return carry

        lax.fori_loop(0, blocks, fill, 0, unroll=2)

    def mix(k, j):
        def multiply(q, carry):
            b = per * q + j
            left = jnp.concatenate([forced[inv[b, place]] for place in range(2)], axis=1)
            both = dot(left, tiles_a[b])
            con[k, b] = both[:rows] + both[rows:]
            return carry

        lax.fori_loop(0, spaces, multiply, 0, unroll=4)

    sums, used = {}, {}

    def partial(i, message):
        m, k, j = message
        r = j // per
        total = con[k, per * space_at(m) + j % per, r * part : (r + 1) * part]
        for child in children.get(message, []):
            sums[i, child].wait_recv()
            total = total + decode(rs_in.at[number(child)])
        return total

    def pass_up(i, message):
        at = number(message)
        total = partial(i, message)
        if message in used:
            used[message].wait_send()
            started[:] = [copy for copy in started if copy is not used[message]]
        encode(total, rs_out.at[at])
        sums[i, message] = used[message] = send(
            rs_out.at[at], rs_in.at[at], rs_s.at[i, at], rs_r.at[i, at], device_at(hops[message])
        )

    def root(i, j):
        r, column = j // per, j % per
        at = (slice(r * part, (r + 1) * part), slice(column * BLOCK, (column + 1) * BLOCK))
        base = control[at].astype(F32)
        terms = partial(i, (0, 0, j))
        if i:
            second_ref[at] = terms
        else:
            first_ref[at] = terms
            encode(base - descent_step * (base + terms), kept(1, 0, 0, j))
            pass_on(1, (0, 0, j))

    far_first = sorted(range(chips), key=lambda k: (-k, k))
    near_first = sorted(range(chips))

    def gathering(i, tasks, roots):
        names = {}
        for message in hops:
            if message in children:
                sends = [((i, child), hops[child]) for child in children[message]]
                tasks[relay, i, message] = (RELAY, [], [(i, message)], sends)
        for k in near_first:
            needs = [(relay, i, (m, k, j)) for m in range(spaces) for j in range(per * PIECES) if (m, k, j) in children and (m or k)]
            takes = [(i, (m, k, j)) for m in range(spaces) for j in range(per * PIECES) if (m, k, j) not in children]
            tasks[spread, i, k] = (SECOND if i else FIRST, needs + roots, takes, [])

    def summing(i, tasks):
        before = []
        for k in far_first:
            tasks[force, i, k] = (FORCE, before, [], [])
            before = []
            for j in range(per):
                tasks[mix, k, j] = (MIX, [(force, i, k)], [], [])
                before.append((mix, k, j))
        for message, hop in hops.items():
            takes = [(i, "sum", child) for child in children.get(message, [])]
            tasks[pass_up, i, message] = (
                CODE + UNCODE * len(takes), [(mix, message[1], message[2] % per)], takes, [((i, "sum", message), hop)]
            )
        for j in range(per * PIECES):
            takes = [(i, "sum", child) for child in children[0, 0, j]]
            sends = [] if i else [((1, child), hops[child]) for child in children[0, 0, j]]
            tasks[root, i, j] = (ROOT, [(mix, 0, j % per)], takes, sends)

    def run(tasks):
        for name in ordered(tasks):
            name[0](*name[1:])

    tables = [(tables_of_tiles,), (tables_of_adjoint,)] + [(build_pick, q) for q in range(nobs // OBS_CHUNK)]
    tasks = {}
    tasks["start",] = (0.0, [], [], [((0, child), hops[child]) for j in range(per * PIECES) for child in children[0, 0, j]])
    for name in tables:
        tasks[name] = (TABLE, [], [], [])
    gathering(0, tasks, [(tables_of_tiles,)])
    for name in ordered(tasks):
        if name != ("start",):
            name[0](*name[1:])
    observe_all(0)
    tasks = {}
    summing(0, tasks)
    gathering(1, tasks, [(root, 0, j) for j in range(per * PIECES)])
    run(tasks)
    observe_all(1)
    tasks = {}
    summing(1, tasks)
    run(tasks)
    for copy in started:
        copy.wait_send()


def per_device(control, block_lists, loc_tiles, ensemble, obs_col, obs_wts, innovation, inv_error):
    rows, width = control.shape
    cells = ensemble.shape[2]
    nobs = obs_col.shape[1]
    spaces, slots = lax.axis_size("space"), lax.axis_size("slot")
    chips = slots // CORES
    per = width // BLOCK
    ncb = spaces * per
    blocks = cells // BLOCK
    messages = per * PIECES * spaces * chips
    part = rows // PIECES
    dma = pltpu.SemaphoreType.DMA
    vmem = pl.BlockSpec(memory_space=pltpu.VMEM)
    out = jax.ShapeDtypeStruct((rows, width), F32)
    first, second = pl.pallas_call(
        functools.partial(kernel, spaces, slots),
        out_shape=(out, out),
        in_specs=[
            vmem, pl.BlockSpec(memory_space=pltpu.SMEM), vmem, pl.BlockSpec(memory_space=pl.ANY),
            vmem, vmem, vmem, vmem,
        ],
        out_specs=(vmem, vmem),
        scratch_shapes=[pltpu.VMEM((ncb, rows, BLOCK), BF16)] * chips
        + [pltpu.VMEM((ncb, rows + PIECES * PAD, BLOCK), I16)] * chips
        + [
            pltpu.VMEM((CORES, chips, rows, cells), BF16),
            pltpu.VMEM((blocks, 2 * BLOCK, BLOCK), BF16),
            pltpu.VMEM((ncb, 2 * BLOCK, BLOCK), BF16),
            pltpu.SMEM((ncb, 2), I32),
            pltpu.VMEM((nobs // OBS_CHUNK, cells, OBS_CHUNK), BF16),
            pltpu.VMEM((nobs // OBS_CHUNK, OBS_CHUNK, cells), BF16),
            pltpu.VMEM((LEV, cells), F32),
            pltpu.VMEM((2, LEV, cells), F32),
            pltpu.VMEM((2, LEV, cells), F32),
            pltpu.VMEM((2 * LEV, cells), BF16),
            pltpu.VMEM((2, LEV, cells), F32),
            pltpu.VMEM((2, LEV, cells), F32),
            pltpu.VMEM((ncb, 2 * rows, BLOCK), BF16),
            pltpu.VMEM((blocks, 2 * rows, BLOCK), BF16),
            pltpu.VMEM((chips, ncb, rows, BLOCK), F32),
            pltpu.VMEM((messages, part + PAD, BLOCK), I16),
            pltpu.VMEM((messages, part + PAD, BLOCK), I16),
            dma((chips,)), dma((chips,)), dma((chips,)),
            dma((2, messages)), dma((2, messages)),
            dma((2, messages)), dma((2, messages)),
            dma((2, 2)), dma((2, 2)),
        ],
        compiler_params=pltpu.CompilerParams(
            collective_id=0, has_side_effects=True, vmem_limit_bytes=58 * 1024 * 1024
        ),
        name="envar_gradients",
    )(
        control, block_lists.T, loc_tiles, ensemble.reshape(slots, rows, cells), obs_col,
        obs_wts, innovation, inv_error,
    )
    base = control.astype(F32)
    first = base + first
    return first, (base - descent_step * first) + second


def solution(mesh):
    placed = (
        P("slot", "space"),
        P("space", None),
        P("space", None, None, None),
        P("slot", None, "space"),
        P("slot", "space"),
        P("slot", None, "space"),
        P("slot", "space"),
        P("slot", "space"),
    )
    return jax.shard_map(
        per_device,
        mesh=mesh,
        in_specs=placed,
        out_specs=(P("slot", "space"), P("slot", "space")),
        check_vma=False,
    )
```

```python
import functools

import jax
import jax.numpy as jnp
from jax import lax
from jax.experimental import pallas as pl
from jax.experimental.pallas import tpu as pltpu
from jax.sharding import PartitionSpec as P

LEV = 48
BLOCK = 128
CORES = 2
OBS_CHUNK = 512
PAD = 16
TOP = 32700.0
FINE = 256.0
descent_step = 0.5
F32 = jnp.float32
BF16 = jnp.bfloat16
I16 = jnp.int16
I32 = jnp.int32
MESH = pl.DeviceIdType.MESH


def halves(x):
    high = x.astype(BF16)
    return high, (x - high.astype(F32)).astype(BF16)


def dot(a, b):
    return lax.dot_general(a, b, (((1,), (0,)), ((), ())), preferred_element_type=F32)


HOP, EXTRA, FLIT = 2.1, 0.5, 1.1
FORCE, MIX, CODE, UNCODE, ROOT, RELAY, FIRST, SECOND, TABLE = 0.45, 0.15, 0.08, 0.03, 0.2, 0.03, 0.7, 1.0, 0.4


def bits_of(m):
    return [1 << i for i in range(m.bit_length()) if m >> i & 1]


PIECES = 1
TREE = ((0, 0, 0, 2, 0, 1, 2, 6, 0, 1, 2, 2, 8, 9, 6, 12), (0, 5, 0, 11, 0, 0, 4, 6, 0, 8, 2, 8, 8, 9, 6, 11))
TREE_UP = ((0, 5, 0, 2, 0, 0, 2, 3, 0, 1, 2, 3, 4, 5, 6, 7), (0, 2, 0, 6, 0, 4, 2, 5, 0, 8, 2, 8, 8, 12, 2, 11))


def tree(spaces, chips, per, table):
    hops, children = {}, {}
    for j in range(per):
        for m in range(spaces):
            for k in range(chips):
                bits = bits_of(m)
                if (spaces, chips, per) == (4, 4, len(table)):
                    above = table[j][m * chips + k]
                    hop = (m ^ above // chips, k ^ above % chips)
                    if not any(hop):
                        continue
                elif k % 2 and (j % 2 or not m):
                    hop = (0, 1)
                elif m:
                    hop = (bits[(len(bits_of(k)) + j) % len(bits)], 0)
                elif k:
                    hop = (0, k)
                else:
                    continue
                hops[m, k, j] = hop
                children.setdefault((m ^ hop[0], k ^ hop[1], j), []).append((m, k, j))
    below = {}

    def height(message):
        if message not in below:
            below[message] = 1 + max([height(child) for child in children.get(message, [])], default=0)
        return below[message]

    for group in children.values():
        group.sort(key=height, reverse=True)
    return hops, children


def arrival(hop, at, links):
    flips, k = hop
    uses = [(bit, FLIT) for bit in bits_of(flips)]
    if k:
        uses.append(("end", FLIT))
    if k > 1:
        uses.append(("middle", 2 * FLIT))
    done = at
    for link, takes in uses:
        at = max(at, links.get(link, 0.0))
        links[link] = at + takes
        done = max(done, links[link])
    return done + HOP + EXTRA * (len(bits_of(flips)) + min(k, 2) - 1)


def ordered(tasks):
    sender = {v: name for name, (_, _, _, sends) in tasks.items() for v, _ in sends}
    hop_of = {v: hop for _, _, _, sends in tasks.values() for v, hop in sends}
    after = {name: [] for name in tasks}
    for name, (_, ends, takes, _) in tasks.items():
        for other in ends:
            after[other].append((name, 0.0))
        for v in takes:
            after[sender[v]].append((name, HOP + FLIT * (1 + (hop_of[v][1] > 1))))
    rest = {}

    def remaining(name):
        if name not in rest:
            rest[name] = tasks[name][0] + max([gap + remaining(v) for v, gap in after[name]], default=0.0)
        return rest[name]

    now, links, ended, there, order = 0.0, {}, {}, {}, []
    left = list(tasks)
    while left:
        ready = {}
        for name in left:
            _, ends, takes, _ = tasks[name]
            if all(v in ended for v in ends) and all(v in there for v in takes):
                ready[name] = max([ended[v] for v in ends] + [there[v] for v in takes], default=0.0)
        able = [v for v in ready if ready[v] <= now]
        if not able:
            now = min(ready.values())
            able = [v for v in ready if ready[v] <= now]
        name = max(able, key=remaining)
        takes_time, _, _, sends = tasks[name]
        now += takes_time
        ended[name] = now
        for v, hop in sends:
            there[v] = arrival(hop, now, links)
        order.append(name)
        left.remove(name)
    return order


def encode(x, ref):
    rows = x.shape[0]
    top = jnp.max(jnp.abs(x), axis=0, keepdims=True)
    log = jnp.ceil(jnp.log2(jnp.maximum(top, 1e-36)) * FINE)
    log = jnp.clip(log, -126.0 * FINE, 126.0 * FINE)
    scale = jnp.exp2(log * (1.0 / FINE)) * (1.0 / TOP)
    ref[:rows] = jnp.round(x * (1.0 / scale)).astype(I32).astype(I16)
    ref[rows : rows + PAD] = jnp.broadcast_to(log, (PAD, BLOCK)).astype(I32).astype(I16)


def decode(ref):
    rows = ref.shape[0] - PAD
    log = ref[rows : rows + PAD].astype(I32).astype(F32)[:1]
    scale = jnp.exp2(log * (1.0 / FINE)) * (1.0 / TOP)
    return ref[:rows].astype(I32).astype(F32) * scale


def kernel(spaces, slots, *refs):
    chips = slots // CORES
    (control, lists, tiles_hbm, ensemble, cols_hbm, wts_hbm, innovation_hbm, inverse_hbm, first_hbm, second_hbm) = refs[:10]
    ctl, coded = refs[10 : 10 + chips], refs[10 + chips : 10 + 2 * chips]
    (
        ens, tiles_t, tiles_a, inv, pick, pick_t, inc, inc_out, inc_in, pair, seen_back, adj, adj_in, split, forced, con,
        rs_out, rs_in, own_s, ens_s, ens_r, ag_s, ag_r, rs_s, rs_r, x_s, x_r,
        tiles, cols, wts, innovation, inverse, outs, io_s,
    ) = refs[10 + 2 * chips :]
    rows, width = control.shape
    per = width // BLOCK
    cells = ensemble.shape[2]
    nobs = cols.shape[1]
    blocks = cells // BLOCK
    listed = lists.shape[0]
    ncb = spaces * per
    members = rows // LEV
    me = lax.axis_index("space")
    slot = lax.axis_index("slot")
    z, core = slot // CORES, lax.rem(slot, CORES)
    sibling = {"slot": slot + 1 - 2 * core}
    part = rows // PIECES
    hops, children = tree(spaces, chips, per * PIECES, TREE)
    hops_up, children_up = tree(spaces, chips, per * PIECES, TREE_UP)

    def flipped(index, flips):
        at = index
        for bit in bits_of(flips):
            at = at + bit * (1 - 2 * lax.rem(index // bit, 2))
        return at

    def space_at(m):
        return flipped(me, m)

    def device_at(hop):
        where = {}
        if hop[0]:
            where["space"] = flipped(me, hop[0])
        if hop[1]:
            where["slot"] = flipped(z, hop[1]) * CORES + core
        return where

    def number(message):
        m, k, j = message
        return (j * spaces + m) * chips + k

    def fetch(src, dst, n):
        copy = pltpu.make_async_copy(src, dst, io_s.at[n])
        copy.start()
        return copy

    mine = [
        fetch(control.at[:, pl.ds(j * BLOCK, BLOCK)], ctl[0].at[per * me + j], j) for j in range(per)
    ]
    barrier = pltpu.get_barrier_semaphore()
    near = [device_at(hop) for hop in sorted({*hops.values(), *hops_up.values()})] + [sibling]
    for where in near:
        pl.semaphore_signal(barrier, inc=1, device_id=where, device_id_type=MESH)
    loads = ((tiles_hbm, tiles), (cols_hbm, cols), (wts_hbm, wts), (innovation_hbm, innovation), (inverse_hbm, inverse))
    loads = [fetch(src, dst, per + n) for n, (src, dst) in enumerate(loads)]
    for copy in mine:
        copy.wait()
    pl.semaphore_wait(barrier, len(near))

    started = []

    def send(src, dst, ssem, rsem, where):
        copy = pltpu.make_async_remote_copy(
            src_ref=src, dst_ref=dst, send_sem=ssem, recv_sem=rsem,
            device_id=where, device_id_type=MESH,
        )
        copy.start()
        started.append(copy)
        return copy

    gathers = {}

    def kept(i, k, m, j):
        at, r = per * space_at(m) + j % per, j // per
        if i:
            return coded[k].at[at, pl.ds(r * (part + PAD), part + PAD)]
        return ctl[k].at[at, pl.ds(r * part, part)]

    def pass_on(i, message):
        m, k, j = message
        for child in children.get(message, []):
            to = number(child)
            gathers[i, child] = send(
                kept(i, k, m, j), kept(i, child[1], m, j), ag_s.at[i, to], ag_r.at[i, to], device_at(hops[child])
            )

    def relay(i, message):
        gathers[i, message].wait_recv()
        pass_on(i, message)

    for j in range(per * PIECES):
        pass_on(0, (0, 0, j))
    moved = {}
    for k in range(chips):
        there = flipped(z, k) * CORES
        moved[k] = [send(ensemble.at[there + 1 - core], ens.at[1, k], ens_s.at[k], ens_r.at[k], sibling).wait_recv]
        own = pltpu.make_async_copy(ensemble.at[there + core], ens.at[0, k], own_s.at[k])
        own.start()
        moved[k].append(own.wait)

    for copy in loads:
        copy.wait()

    def build_tiles(g, carry):
        for e in range(listed):
            tiles_t[g, e * BLOCK : (e + 1) * BLOCK] = tiles[g, e].astype(F32).T.astype(BF16)
        return carry

    def build_adjoint(b, carry):
        one, two = jnp.int32(-1), jnp.int32(-1)
        for g in range(blocks):
            for e in range(listed):
                hit = lists[e, g] == b
                two = jnp.where(hit, jnp.where(one >= 0, g * listed + e, two), two)
                one = jnp.where(hit, jnp.where(one >= 0, one, g * listed + e), one)
        for place, found in enumerate((one, two)):
            kept = jnp.where(found >= 0, 1.0, 0.0)
            found = jnp.maximum(found, 0)
            g = found // listed
            inv[b, place] = g
            tile = tiles[g, lax.rem(found, listed)].astype(F32) * kept
            tiles_a[b, place * BLOCK : (place + 1) * BLOCK] = tile.astype(BF16)
        return carry

    first_cell = me * cells

    def build_pick(q):
        line = cols[:, q * OBS_CHUNK : (q + 1) * OBS_CHUNK] - first_cell

        def band(r, carry):
            rowid = lax.broadcasted_iota(I32, (BLOCK, OBS_CHUNK), 0) + r * BLOCK
            at = pl.ds(pl.multiple_of(r * BLOCK, BLOCK), BLOCK)
            pick[q, at] = jnp.where(rowid == line, 1.0, 0.0).astype(BF16)
            return carry

        lax.fori_loop(0, blocks, band, 0)
        turned = [
            jnp.broadcast_to(line[:, h * BLOCK : (h + 1) * BLOCK].astype(F32), (BLOCK, BLOCK)).T
            for h in range(OBS_CHUNK // BLOCK)
        ]

        def band_t(r, carry):
            lane = (lax.broadcasted_iota(I32, (BLOCK, BLOCK), 1) + r * BLOCK).astype(F32)
            at = pl.ds(pl.multiple_of(r * BLOCK, BLOCK), BLOCK)
            for h, column in enumerate(turned):
                pick_t[q * OBS_CHUNK + h * BLOCK : q * OBS_CHUNK + (h + 1) * BLOCK, at] = jnp.where(column == lane, 1.0, 0.0).astype(BF16)
            return carry

        lax.fori_loop(0, blocks, band_t, 0)

    def tables_of_tiles():
        lax.fori_loop(0, blocks, build_tiles, 0)

    def tables_of_adjoint():
        lax.fori_loop(0, ncb, build_adjoint, 0)

    def member(n):
        return slice(n * LEV, (n + 1) * LEV)

    def lanes(g):
        return pl.ds(pl.multiple_of(g * BLOCK, BLOCK), BLOCK)

    spread_yet = set()
    swaps = {}

    def spread(i, k):
        fresh = i not in spread_yet
        spread_yet.add(i)
        for m in range(spaces):
            for j in range(per * PIECES):
                if (m or k) and (m, k, j) not in children:
                    gathers[i, (m, k, j)].wait_recv()
        if not i:
            for arrive in moved[k]:
                arrive()
        if i:

            def unpack(b, carry):
                for r in range(PIECES):
                    at = r * (part + PAD)
                    up, down = halves(decode(coded[k].at[b, at : at + part + PAD]))
                    split[b, r * part : (r + 1) * part] = up
                    split[b, rows + r * part : rows + (r + 1) * part] = down
                return carry

            lax.fori_loop(0, ncb, unpack, 0, unroll=2)

        def run(g, carry):
            held = split if i else ctl[k]
            left = jnp.concatenate([held[lists[e, g]] for e in range(listed)], axis=1)
            value = dot(left, tiles_t[g])
            if i:
                value = value[:rows] + value[rows:]
            at = lanes(g)
            for s, target in enumerate((inc, inc_out.at[i])):
                total = None if fresh else target[:, at]
                for n in range(members):
                    term = ens[s, k, member(n), at].astype(F32) * value[member(n)]
                    total = term if total is None else total + term
                target[:, at] = total
            return carry

        lax.fori_loop(0, blocks, run, 0, unroll=4)

    def observe_all(i):
        swap = send(inc_out.at[i], inc_in.at[i], x_s.at[i, 0], x_r.at[i, 0], sibling)
        swap.wait_recv()
        high, low = halves(inc[...] + inc_in[i])
        pair[:LEV] = high
        pair[LEV:] = low

        def observe(q, carry):
            at = pl.ds(pl.multiple_of(q * OBS_CHUNK, OBS_CHUNK), OBS_CHUNK)
            seen = dot(pair[...], pick[q])
            seen = seen[:LEV] + seen[LEV:]
            w = wts[0, :, at]
            modelled = jnp.sum(w * seen, axis=0, keepdims=True)
            residual = inverse[:, at] * (modelled - innovation[:, at])
            up, down = halves(w * residual)
            seen_back[:LEV, at] = up
            seen_back[LEV:, at] = down
            return carry

        lax.fori_loop(0, nobs // OBS_CHUNK, observe, 0, unroll=True)
        for h in range(2):
            at = slice(h * cells // 2, (h + 1) * cells // 2)
            back = dot(seen_back[...], pick_t[:, at])
            adj[i, h] = back[:LEV] + back[LEV:]
            swaps[i, h] = send(adj.at[i, h], adj_in.at[i, h], x_s.at[i, 1 + h], x_r.at[i, 1 + h], sibling)

    def force(i, k):
        for h in range(2):
            if (i, h) in swaps:
                swaps.pop((i, h)).wait_recv()

            def fill(g, carry):
                at = lanes(g)
                near = pl.ds(pl.multiple_of((g - h * (blocks // 2)) * BLOCK, BLOCK), BLOCK)
                mine, other = adj[i, h, :, near], adj_in[i, h, :, near]
                for n in range(members):
                    total = ens[0, k, member(n), at].astype(F32) * mine + ens[1, k, member(n), at].astype(F32) * other
                    up, down = halves(total)
                    forced[g, member(n)] = up
                    forced[g, rows + n * LEV : rows + (n + 1) * LEV] = down
                return carry

            lax.fori_loop(h * (blocks // 2), (h + 1) * (blocks // 2), fill, 0, unroll=2)

    def mix(k, j):
        def multiply(q, carry):
            b = per * q + j
            left = jnp.concatenate([forced[inv[b, place]] for place in range(2)], axis=1)
            both = dot(left, tiles_a[b])
            con[k, b] = both[:rows] + both[rows:]
            return carry

        lax.fori_loop(0, spaces, multiply, 0, unroll=4)

    sums, used = {}, {}

    def partial(i, message):
        m, k, j = message
        r = j // per
        total = con[k, per * space_at(m) + j % per, r * part : (r + 1) * part]
        for child in children_up.get(message, []):
            sums[i, child].wait_recv()
            total = total + decode(rs_in.at[number(child)])
        return total

    def pass_up(i, message):
        at = number(message)
        total = partial(i, message)
        if message in used:
            used[message].wait_send()
            started[:] = [copy for copy in started if copy is not used[message]]
        encode(total, rs_out.at[at])
        sums[i, message] = used[message] = send(
            rs_out.at[at], rs_in.at[at], rs_s.at[i, at], rs_r.at[i, at], device_at(hops_up[message])
        )

    def root(i, j):
        r, column = j // per, j % per
        band = slice(r * part, (r + 1) * part)
        base = ctl[0][per * me + column, band].astype(F32)
        terms = partial(i, (0, 0, j))
        outs[i, column, band] = terms
        out = (second_hbm if i else first_hbm).at[pl.ds(r * part, part), pl.ds(column * BLOCK, BLOCK)]
        written.append(fetch(outs.at[i, column, pl.ds(r * part, part)], out, per + 5 + i * per * PIECES + j))
        if not i:
            encode(base - descent_step * (base + terms), kept(1, 0, 0, j))
            pass_on(1, (0, 0, j))

    written = []
    far_first = sorted(range(chips), key=lambda k: (-k, k))
    near_first = sorted(range(chips))

    def gathering(i, tasks, roots):
        names = {}
        for message in hops:
            if message in children:
                sends = [((i, child), hops[child]) for child in children[message]]
                tasks[relay, i, message] = (RELAY, [], [(i, message)], sends)
        for k in near_first:
            needs = [(relay, i, (m, k, j)) for m in range(spaces) for j in range(per * PIECES) if (m, k, j) in children and (m or k)]
            takes = [(i, (m, k, j)) for m in range(spaces) for j in range(per * PIECES) if (m, k, j) not in children]
            tasks[spread, i, k] = (SECOND if i else FIRST, needs + roots, takes, [])

    def summing(i, tasks):
        before = []
        for k in far_first:
            tasks[force, i, k] = (FORCE, before, [], [])
            before = []
            for j in range(per):
                tasks[mix, k, j] = (MIX, [(force, i, k)], [], [])
                before.append((mix, k, j))
        for message, hop in hops_up.items():
            takes = [(i, "sum", child) for child in children_up.get(message, [])]
            tasks[pass_up, i, message] = (
                CODE + UNCODE * len(takes), [(mix, message[1], message[2] % per)], takes, [((i, "sum", message), hop)]
            )
        for j in range(per * PIECES):
            takes = [(i, "sum", child) for child in children_up[0, 0, j]]
            sends = [] if i else [((1, child), hops[child]) for child in children[0, 0, j]]
            tasks[root, i, j] = (ROOT, [(mix, 0, j % per)], takes, sends)

    def run(tasks):
        for name in ordered(tasks):
            name[0](*name[1:])

    tables = [(tables_of_tiles,), (tables_of_adjoint,)] + [(build_pick, q) for q in range(nobs // OBS_CHUNK)]
    tasks = {}
    tasks["start",] = (0.0, [], [], [((0, child), hops[child]) for j in range(per * PIECES) for child in children[0, 0, j]])
    for name in tables:
        tasks[name] = (TABLE, [], [], [])
    gathering(0, tasks, [(tables_of_tiles,)])
    for name in ordered(tasks):
        if name != ("start",):
            name[0](*name[1:])
    observe_all(0)
    tasks = {}
    summing(0, tasks)
    gathering(1, tasks, [(root, 0, j) for j in range(per * PIECES)])
    run(tasks)
    observe_all(1)
    tasks = {}
    summing(1, tasks)
    run(tasks)
    for copy in started:
        copy.wait_send()
    for copy in written:
        copy.wait()


def per_device(control, block_lists, loc_tiles, ensemble, obs_col, obs_wts, innovation, inv_error):
    rows, width = control.shape
    cells = ensemble.shape[2]
    nobs = obs_col.shape[1]
    spaces, slots = lax.axis_size("space"), lax.axis_size("slot")
    chips = slots // CORES
    per = width // BLOCK
    ncb = spaces * per
    blocks = cells // BLOCK
    messages = per * PIECES * spaces * chips
    part = rows // PIECES
    dma = pltpu.SemaphoreType.DMA
    hbm = pl.BlockSpec(memory_space=pl.ANY)
    out = jax.ShapeDtypeStruct((rows, width), F32)
    first, second = pl.pallas_call(
        functools.partial(kernel, spaces, slots),
        out_shape=(out, out),
        in_specs=[
            hbm, pl.BlockSpec(memory_space=pltpu.SMEM), hbm, hbm, hbm, hbm, hbm, hbm,
        ],
        out_specs=(hbm, hbm),
        scratch_shapes=[pltpu.VMEM((ncb, rows, BLOCK), BF16)] * chips
        + [pltpu.VMEM((ncb, rows + PIECES * PAD, BLOCK), I16)] * chips
        + [
            pltpu.VMEM((CORES, chips, rows, cells), BF16),
            pltpu.VMEM((blocks, 2 * BLOCK, BLOCK), BF16),
            pltpu.VMEM((ncb, 2 * BLOCK, BLOCK), BF16),
            pltpu.SMEM((ncb, 2), I32),
            pltpu.VMEM((nobs // OBS_CHUNK, cells, OBS_CHUNK), BF16),
            pltpu.VMEM((nobs, cells), BF16),
            pltpu.VMEM((LEV, cells), F32),
            pltpu.VMEM((2, LEV, cells), F32),
            pltpu.VMEM((2, LEV, cells), F32),
            pltpu.VMEM((2 * LEV, cells), BF16),
            pltpu.VMEM((2 * LEV, nobs), BF16),
            pltpu.VMEM((2, 2, LEV, cells // 2), F32),
            pltpu.VMEM((2, 2, LEV, cells // 2), F32),
            pltpu.VMEM((ncb, 2 * rows, BLOCK), BF16),
            pltpu.VMEM((blocks, 2 * rows, BLOCK), BF16),
            pltpu.VMEM((chips, ncb, rows, BLOCK), F32),
            pltpu.VMEM((messages, part + PAD, BLOCK), I16),
            pltpu.VMEM((messages, part + PAD, BLOCK), I16),
            dma((chips,)), dma((chips,)), dma((chips,)),
            dma((2, messages)), dma((2, messages)),
            dma((2, messages)), dma((2, messages)),
            dma((2, 3)), dma((2, 3)),
            pltpu.VMEM(loc_tiles.shape, BF16),
            pltpu.VMEM(obs_col.shape, I32),
            pltpu.VMEM(obs_wts.shape, F32),
            pltpu.VMEM(innovation.shape, F32),
            pltpu.VMEM(inv_error.shape, F32),
            pltpu.VMEM((2, per, rows, BLOCK), F32),
            dma((5 + per + 2 * per * PIECES,)),
        ],
        compiler_params=pltpu.CompilerParams(
            collective_id=0, has_side_effects=True, vmem_limit_bytes=58 * 1024 * 1024
        ),
        name="envar_gradients",
    )(
        control, block_lists.T, loc_tiles, ensemble.reshape(slots, rows, cells), obs_col,
        obs_wts, innovation, inv_error,
    )
    base = control.astype(F32)
    first = base + first
    return first, (base - descent_step * first) + second


def solution(mesh):
    placed = (
        P("slot", "space"),
        P("space", None),
        P("space", None, None, None),
        P("slot", None, "space"),
        P("slot", "space"),
        P("slot", None, "space"),
        P("slot", "space"),
        P("slot", "space"),
    )
    return jax.shard_map(
        per_device,
        mesh=mesh,
        in_specs=placed,
        out_specs=(P("slot", "space"), P("slot", "space")),
        check_vma=False,
    )
```

```python
import functools

import jax
import jax.numpy as jnp
from jax import lax
from jax.experimental import pallas as pl
from jax.experimental.pallas import tpu as pltpu
from jax.sharding import PartitionSpec as P

LEV = 48
BLOCK = 128
CORES = 2
OBS_CHUNK = 1024
TOP = 32700.0
descent_step = 0.5
F32 = jnp.float32
BF16 = jnp.bfloat16
I16 = jnp.int16
I32 = jnp.int32
MESH = pl.DeviceIdType.MESH


def halves(x):
    high = x.astype(BF16)
    return high, (x - high.astype(F32)).astype(BF16)


def dot(a, b):
    return lax.dot_general(a, b, (((1,), (0,)), ((), ())), preferred_element_type=F32)


HOP, EXTRA, FLIT = 2.8, 0.5, 1.03
FORCE, MIX, CODE, UNCODE, ROOT, RELAY, FIRST, SECOND, TABLE = 0.45, 0.15, 0.08, 0.03, 0.2, 0.03, 0.7, 1.0, 0.4


def bits_of(m):
    return [1 << i for i in range(m.bit_length()) if m >> i & 1]


PIECES = 1
TREE = ((0, 0, 0, 2, 0, 1, 2, 3, 0, 1, 2, 3, 4, 5, 6, 12), (0, 2, 0, 2, 0, 4, 2, 3, 0, 8, 2, 8, 8, 9, 6, 11))
TREE_UP = ((0, 0, 0, 2, 0, 1, 2, 3, 0, 1, 2, 3, 4, 5, 6, 12), (0, 2, 0, 2, 0, 4, 2, 3, 0, 8, 2, 8, 8, 9, 6, 11))


def tree(spaces, chips, per, table):
    hops, children = {}, {}
    for j in range(per):
        for m in range(spaces):
            for k in range(chips):
                bits = bits_of(m)
                if (spaces, chips, per) == (4, 4, len(table)):
                    above = table[j][m * chips + k]
                    hop = (m ^ above // chips, k ^ above % chips)
                    if not any(hop):
                        continue
                elif k % 2 and (j % 2 or not m):
                    hop = (0, 1)
                elif m:
                    hop = (bits[(len(bits_of(k)) + j) % len(bits)], 0)
                elif k:
                    hop = (0, k)
                else:
                    continue
                hops[m, k, j] = hop
                children.setdefault((m ^ hop[0], k ^ hop[1], j), []).append((m, k, j))
    below = {}

    def height(message):
        if message not in below:
            below[message] = 1 + max([height(child) for child in children.get(message, [])], default=0)
        return below[message]

    for group in children.values():
        group.sort(key=height, reverse=True)
    return hops, children


def arrival(hop, at, links):
    flips, k = hop
    uses = [(bit, FLIT) for bit in bits_of(flips)]
    if k:
        uses.append(("end", FLIT))
    if k > 1:
        uses.append(("middle", 2 * FLIT))
    done = at
    for link, takes in uses:
        at = max(at, links.get(link, 0.0))
        links[link] = at + takes
        done = max(done, links[link])
    return done + HOP + EXTRA * (len(bits_of(flips)) + min(k, 2) - 1)


SALTS = (0, 0, 0)
AMP = 0.15


def ordered(tasks, salt):
    sender = {v: name for name, (_, _, _, sends) in tasks.items() for v, _ in sends}
    hop_of = {v: hop for _, _, _, sends in tasks.values() for v, hop in sends}
    after = {name: [] for name in tasks}
    for name, (_, ends, takes, _) in tasks.items():
        for other in ends:
            after[other].append((name, 0.0))
        for v in takes:
            after[sender[v]].append((name, HOP + FLIT * (1 + (hop_of[v][1] > 1))))
    rest = {}

    def remaining(name):
        if name not in rest:
            rest[name] = tasks[name][0] + max([gap + remaining(v) for v, gap in after[name]], default=0.0)
        return rest[name]

    place = {name: n for n, name in enumerate(tasks)}

    def weight(name):
        shift = ((place[name] + 1) * (salt * 7919 + 104729) % 10007) / 10007 if salt else 0.5
        return remaining(name) * (1.0 + AMP * (shift - 0.5))

    now, links, ended, there, order = 0.0, {}, {}, {}, []
    left = list(tasks)
    while left:
        ready = {}
        for name in left:
            _, ends, takes, _ = tasks[name]
            if all(v in ended for v in ends) and all(v in there for v in takes):
                ready[name] = max([ended[v] for v in ends] + [there[v] for v in takes], default=0.0)
        able = [v for v in ready if ready[v] <= now]
        if not able:
            now = min(ready.values())
            able = [v for v in ready if ready[v] <= now]
        name = max(able, key=weight)
        takes_time, _, _, sends = tasks[name]
        now += takes_time
        ended[name] = now
        for v, hop in sends:
            there[v] = arrival(hop, now, links)
        order.append(name)
        left.remove(name)
    return order


def encode(x, ref, unit):
    top = jnp.max(jnp.abs(x), axis=0, keepdims=True)
    scale = jnp.maximum(top, 1e-30) * (1.0 / TOP)
    unit[...] = scale
    ref[...] = jnp.round(x * (1.0 / scale)).astype(I32).astype(I16)


def decode(ref, unit):
    return ref[...].astype(I32).astype(F32) * unit[...]


def kernel(spaces, slots, *refs):
    chips = slots // CORES
    (control, lists, tiles_hbm, ensemble, cols_hbm, wts_hbm, innovation_hbm, inverse_hbm, first_hbm, second_hbm) = refs[:10]
    ctl, coded, units = (refs[10 + n * chips : 10 + (n + 1) * chips] for n in range(3))
    (
        ens, tiles_t, tiles_a, inv, pick, pick_t, inc, inc_out, inc_in, pair, seen_back, adj, adj_in, split, forced, con,
        rs_out, rs_in, out_unit, in_unit, own_s, ens_s, ens_r, ag_s, ag_r, au_s, au_r, rs_s, rs_r, ru_s, ru_r, x_s, x_r,
        tiles, cols, wts, innovation, inverse, outs, io_s,
    ) = refs[10 + 3 * chips :]
    rows, width = control.shape
    per = width // BLOCK
    cells = ensemble.shape[2]
    nobs = cols.shape[1]
    blocks = cells // BLOCK
    listed = lists.shape[0]
    ncb = spaces * per
    members = rows // LEV
    me = lax.axis_index("space")
    slot = lax.axis_index("slot")
    z, core = slot // CORES, lax.rem(slot, CORES)
    sibling = {"slot": slot + 1 - 2 * core}
    part = rows // PIECES
    hops, children = tree(spaces, chips, per * PIECES, TREE)
    hops_up, children_up = tree(spaces, chips, per * PIECES, TREE_UP)

    def flipped(index, flips):
        at = index
        for bit in bits_of(flips):
            at = at + bit * (1 - 2 * lax.rem(index // bit, 2))
        return at

    def space_at(m):
        return flipped(me, m)

    def device_at(hop):
        where = {}
        if hop[0]:
            where["space"] = flipped(me, hop[0])
        if hop[1]:
            where["slot"] = flipped(z, hop[1]) * CORES + core
        return where

    def number(message):
        m, k, j = message
        return (j * spaces + m) * chips + k

    def fetch(src, dst, n):
        copy = pltpu.make_async_copy(src, dst, io_s.at[n])
        copy.start()
        return copy

    mine = [
        fetch(control.at[:, pl.ds(j * BLOCK, BLOCK)], ctl[0].at[per * me + j], j) for j in range(per)
    ]
    barrier = pltpu.get_barrier_semaphore()
    near = [device_at(hop) for hop in sorted({*hops.values(), *hops_up.values()})] + [sibling]
    for where in near:
        pl.semaphore_signal(barrier, inc=1, device_id=where, device_id_type=MESH)
    loads = ((tiles_hbm, tiles), (cols_hbm, cols), (wts_hbm, wts), (innovation_hbm, innovation), (inverse_hbm, inverse))
    loads = [fetch(src, dst, per + n) for n, (src, dst) in enumerate(loads)]
    for copy in mine:
        copy.wait()
    pl.semaphore_wait(barrier, len(near))

    started = []

    def send(src, dst, ssem, rsem, where):
        copy = pltpu.make_async_remote_copy(
            src_ref=src, dst_ref=dst, send_sem=ssem, recv_sem=rsem,
            device_id=where, device_id_type=MESH,
        )
        copy.start()
        started.append(copy)
        return copy

    gathers = {}

    def kept(i, k, m, j):
        at, r = per * space_at(m) + j % per, j // per
        return (coded if i else ctl)[k].at[at, pl.ds(r * part, part)]

    def unit_of(k, m, j):
        return units[k].at[per * space_at(m) + j % per, j // per]

    def pass_on(i, message):
        m, k, j = message
        for child in children.get(message, []):
            to = number(child)
            where = device_at(hops[child])
            gathers[i, child] = [
                send(kept(i, k, m, j), kept(i, child[1], m, j), ag_s.at[i, to], ag_r.at[i, to], where)
            ]
            if i:
                gathers[i, child].append(
                    send(unit_of(k, m, j), unit_of(child[1], m, j), au_s.at[to], au_r.at[to], where)
                )

    def relay(i, message):
        for copy in gathers[i, message]:
            copy.wait_recv()
        pass_on(i, message)

    for j in range(per * PIECES):
        pass_on(0, (0, 0, j))
    moved = {}
    for k in range(chips):
        there = flipped(z, k) * CORES
        moved[k] = [send(ensemble.at[there + 1 - core], ens.at[1, k], ens_s.at[k], ens_r.at[k], sibling).wait_recv]
        own = pltpu.make_async_copy(ensemble.at[there + core], ens.at[0, k], own_s.at[k])
        own.start()
        moved[k].append(own.wait)

    for copy in loads:
        copy.wait()

    def build_tiles(g, carry):
        for e in range(listed):
            tiles_t[g, e * BLOCK : (e + 1) * BLOCK] = tiles[g, e].astype(F32).T.astype(BF16)
        return carry

    def build_adjoint(b, carry):
        one, two = jnp.int32(-1), jnp.int32(-1)
        for g in range(blocks):
            for e in range(listed):
                hit = lists[e, g] == b
                two = jnp.where(hit, jnp.where(one >= 0, g * listed + e, two), two)
                one = jnp.where(hit, jnp.where(one >= 0, one, g * listed + e), one)
        for place, found in enumerate((one, two)):
            kept = jnp.where(found >= 0, 1.0, 0.0)
            found = jnp.maximum(found, 0)
            g = found // listed
            inv[b, place] = g
            tile = tiles[g, lax.rem(found, listed)].astype(F32) * kept
            tiles_a[b, place * BLOCK : (place + 1) * BLOCK] = tile.astype(BF16)
        return carry

    first_cell = me * cells

    def build_pick(q):
        line = cols[:, q * OBS_CHUNK : (q + 1) * OBS_CHUNK] - first_cell

        def band(r, carry):
            rowid = lax.broadcasted_iota(I32, (BLOCK, OBS_CHUNK), 0) + r * BLOCK
            at = pl.ds(pl.multiple_of(r * BLOCK, BLOCK), BLOCK)
            pick[q, at] = jnp.where(rowid == line, 1.0, 0.0).astype(BF16)
            return carry

        lax.fori_loop(0, blocks, band, 0)
        turned = [
            jnp.broadcast_to(line[:, h * BLOCK : (h + 1) * BLOCK].astype(F32), (BLOCK, BLOCK)).T
            for h in range(OBS_CHUNK // BLOCK)
        ]

        def band_t(r, carry):
            lane = (lax.broadcasted_iota(I32, (BLOCK, BLOCK), 1) + r * BLOCK).astype(F32)
            at = pl.ds(pl.multiple_of(r * BLOCK, BLOCK), BLOCK)
            for h, column in enumerate(turned):
                pick_t[q * OBS_CHUNK + h * BLOCK : q * OBS_CHUNK + (h + 1) * BLOCK, at] = jnp.where(column == lane, 1.0, 0.0).astype(BF16)
            return carry

        lax.fori_loop(0, blocks, band_t, 0)

    def tables_of_tiles():
        lax.fori_loop(0, blocks, build_tiles, 0)

    def tables_of_adjoint():
        lax.fori_loop(0, ncb, build_adjoint, 0)

    def member(n):
        return slice(n * LEV, (n + 1) * LEV)

    def lanes(g):
        return pl.ds(pl.multiple_of(g * BLOCK, BLOCK), BLOCK)

    spread_yet = set()
    swaps = {}

    def spread(i, k):
        fresh = i not in spread_yet
        spread_yet.add(i)
        for m in range(spaces):
            for j in range(per * PIECES):
                if (m or k) and (m, k, j) not in children:
                    for copy in gathers[i, (m, k, j)]:
                        copy.wait_recv()
        if not i:
            for arrive in moved[k]:
                arrive()
        if i:

            def unpack(b, carry):
                for r in range(PIECES):
                    up, down = halves(decode(coded[k].at[b, r * part : (r + 1) * part], units[k].at[b, r]))
                    split[b, r * part : (r + 1) * part] = up
                    split[b, rows + r * part : rows + (r + 1) * part] = down
                return carry

            lax.fori_loop(0, ncb, unpack, 0, unroll=2)

        def run(g, carry):
            held = split if i else ctl[k]
            left = jnp.concatenate([held[lists[e, g]] for e in range(listed)], axis=1)
            value = dot(left, tiles_t[g])
            if i:
                value = value[:rows] + value[rows:]
            at = lanes(g)
            for s, target in enumerate((inc, inc_out.at[i])):
                total = None if fresh else target[:, at]
                for n in range(members):
                    term = ens[s, k, member(n), at].astype(F32) * value[member(n)]
                    total = term if total is None else total + term
                target[:, at] = total
            return carry

        lax.fori_loop(0, blocks, run, 0, unroll=4)

    def observe_all(i):
        swap = send(inc_out.at[i], inc_in.at[i], x_s.at[i, 0], x_r.at[i, 0], sibling)
        swap.wait_recv()
        high, low = halves(inc[...] + inc_in[i])
        pair[:LEV] = high
        pair[LEV:] = low

        def observe(q, carry):
            at = pl.ds(pl.multiple_of(q * OBS_CHUNK, OBS_CHUNK), OBS_CHUNK)
            seen = dot(pair[...], pick[q])
            seen = seen[:LEV] + seen[LEV:]
            w = wts[0, :, at]
            modelled = jnp.sum(w * seen, axis=0, keepdims=True)
            residual = inverse[:, at] * (modelled - innovation[:, at])
            up, down = halves(w * residual)
            seen_back[:LEV, at] = up
            seen_back[LEV:, at] = down
            return carry

        lax.fori_loop(0, nobs // OBS_CHUNK, observe, 0, unroll=True)
        for h in range(2):
            at = slice(h * cells // 2, (h + 1) * cells // 2)
            back = dot(seen_back[...], pick_t[:, at])
            adj[i, h] = back[:LEV] + back[LEV:]
            swaps[i, h] = send(adj.at[i, h], adj_in.at[i, h], x_s.at[i, 1 + h], x_r.at[i, 1 + h], sibling)

    def force(i, k):
        for h in range(2):
            if (i, h) in swaps:
                swaps.pop((i, h)).wait_recv()

            def fill(g, carry):
                at = lanes(g)
                near = pl.ds(pl.multiple_of((g - h * (blocks // 2)) * BLOCK, BLOCK), BLOCK)
                mine, other = adj[i, h, :, near], adj_in[i, h, :, near]
                for n in range(members):
                    total = ens[0, k, member(n), at].astype(F32) * mine + ens[1, k, member(n), at].astype(F32) * other
                    up, down = halves(total)
                    forced[g, member(n)] = up
                    forced[g, rows + n * LEV : rows + (n + 1) * LEV] = down
                return carry

            lax.fori_loop(h * (blocks // 2), (h + 1) * (blocks // 2), fill, 0, unroll=2)

    def mix(k, j):
        def multiply(q, carry):
            b = per * q + j
            left = jnp.concatenate([forced[inv[b, place]] for place in range(2)], axis=1)
            both = dot(left, tiles_a[b])
            con[k, b] = both[:rows] + both[rows:]
            return carry

        lax.fori_loop(0, spaces, multiply, 0, unroll=4)

    sums, used = {}, {}

    def partial(i, message):
        m, k, j = message
        r = j // per
        total = con[k, per * space_at(m) + j % per, r * part : (r + 1) * part]
        for child in children_up.get(message, []):
            for copy in sums[i, child]:
                copy.wait_recv()
            total = total + decode(rs_in.at[number(child)], in_unit.at[number(child)])
        return total

    def pass_up(i, message):
        at = number(message)
        total = partial(i, message)
        if message in used:
            for old in used[message]:
                old.wait_send()
                started[:] = [copy for copy in started if copy is not old]
        encode(total, rs_out.at[at], out_unit.at[at])
        where = device_at(hops_up[message])
        sums[i, message] = used[message] = [
            send(out_unit.at[at], in_unit.at[at], ru_s.at[i, at], ru_r.at[i, at], where),
            send(rs_out.at[at], rs_in.at[at], rs_s.at[i, at], rs_r.at[i, at], where),
        ]

    def root(i, j):
        r, column = j // per, j % per
        band = slice(r * part, (r + 1) * part)
        base = ctl[0][per * me + column, band].astype(F32)
        terms = partial(i, (0, 0, j))
        outs[i, column, band] = terms
        out = (second_hbm if i else first_hbm).at[pl.ds(r * part, part), pl.ds(column * BLOCK, BLOCK)]
        written.append(fetch(outs.at[i, column, pl.ds(r * part, part)], out, per + 5 + i * per * PIECES + j))
        if not i:
            encode(base - descent_step * (base + terms), kept(1, 0, 0, j), unit_of(0, 0, j))
            pass_on(1, (0, 0, j))

    written = []
    far_first = sorted(range(chips), key=lambda k: (-k, k))
    near_first = sorted(range(chips))

    def gathering(i, tasks, roots):
        names = {}
        for message in hops:
            if message in children:
                sends = [((i, child), hops[child]) for child in children[message]]
                tasks[relay, i, message] = (RELAY, [], [(i, message)], sends)
        for k in near_first:
            needs = [(relay, i, (m, k, j)) for m in range(spaces) for j in range(per * PIECES) if (m, k, j) in children and (m or k)]
            takes = [(i, (m, k, j)) for m in range(spaces) for j in range(per * PIECES) if (m, k, j) not in children]
            tasks[spread, i, k] = (SECOND if i else FIRST, needs + roots, takes, [])

    def summing(i, tasks):
        before = []
        for k in far_first:
            tasks[force, i, k] = (FORCE, before, [], [])
            before = []
            for j in range(per):
                tasks[mix, k, j] = (MIX, [(force, i, k)], [], [])
                before.append((mix, k, j))
        for message, hop in hops_up.items():
            takes = [(i, "sum", child) for child in children_up.get(message, [])]
            tasks[pass_up, i, message] = (
                CODE + UNCODE * len(takes), [(mix, message[1], message[2] % per)], takes, [((i, "sum", message), hop)]
            )
        for j in range(per * PIECES):
            takes = [(i, "sum", child) for child in children_up[0, 0, j]]
            sends = [] if i else [((1, child), hops[child]) for child in children[0, 0, j]]
            tasks[root, i, j] = (ROOT, [(mix, 0, j % per)], takes, sends)

    def run(tasks, salt):
        for name in ordered(tasks, salt):
            name[0](*name[1:])

    tables = [(tables_of_tiles,), (tables_of_adjoint,)] + [(build_pick, q) for q in range(nobs // OBS_CHUNK)]
    tasks = {}
    tasks["start",] = (0.0, [], [], [((0, child), hops[child]) for j in range(per * PIECES) for child in children[0, 0, j]])
    for name in tables:
        tasks[name] = (TABLE, [], [], [])
    gathering(0, tasks, [(tables_of_tiles,)])
    for name in ordered(tasks, SALTS[0]):
        if name != ("start",):
            name[0](*name[1:])
    observe_all(0)
    tasks = {}
    summing(0, tasks)
    gathering(1, tasks, [(root, 0, j) for j in range(per * PIECES)])
    run(tasks, SALTS[1])
    observe_all(1)
    tasks = {}
    summing(1, tasks)
    run(tasks, SALTS[2])
    for copy in started:
        copy.wait_send()
    for copy in written:
        copy.wait()


def per_device(control, block_lists, loc_tiles, ensemble, obs_col, obs_wts, innovation, inv_error):
    rows, width = control.shape
    cells = ensemble.shape[2]
    nobs = obs_col.shape[1]
    spaces, slots = lax.axis_size("space"), lax.axis_size("slot")
    chips = slots // CORES
    per = width // BLOCK
    ncb = spaces * per
    blocks = cells // BLOCK
    messages = per * PIECES * spaces * chips
    part = rows // PIECES
    dma = pltpu.SemaphoreType.DMA
    hbm = pl.BlockSpec(memory_space=pl.ANY)
    out = jax.ShapeDtypeStruct((rows, width), F32)
    first, second = pl.pallas_call(
        functools.partial(kernel, spaces, slots),
        out_shape=(out, out),
        in_specs=[
            hbm, pl.BlockSpec(memory_space=pltpu.SMEM), hbm, hbm, hbm, hbm, hbm, hbm,
        ],
        out_specs=(hbm, hbm),
        scratch_shapes=[pltpu.VMEM((ncb, rows, BLOCK), BF16)] * chips
        + [pltpu.VMEM((ncb, rows, BLOCK), I16)] * chips
        + [pltpu.VMEM((ncb, PIECES, 1, BLOCK), F32)] * chips
        + [
            pltpu.VMEM((CORES, chips, rows, cells), BF16),
            pltpu.VMEM((blocks, 2 * BLOCK, BLOCK), BF16),
            pltpu.VMEM((ncb, 2 * BLOCK, BLOCK), BF16),
            pltpu.SMEM((ncb, 2), I32),
            pltpu.VMEM((nobs // OBS_CHUNK, cells, OBS_CHUNK), BF16),
            pltpu.VMEM((nobs, cells), BF16),
            pltpu.VMEM((LEV, cells), F32),
            pltpu.VMEM((2, LEV, cells), F32),
            pltpu.VMEM((2, LEV, cells), F32),
            pltpu.VMEM((2 * LEV, cells), BF16),
            pltpu.VMEM((2 * LEV, nobs), BF16),
            pltpu.VMEM((2, 2, LEV, cells // 2), F32),
            pltpu.VMEM((2, 2, LEV, cells // 2), F32),
            pltpu.VMEM((ncb, 2 * rows, BLOCK), BF16),
            pltpu.VMEM((blocks, 2 * rows, BLOCK), BF16),
            pltpu.VMEM((chips, ncb, rows, BLOCK), F32),
            pltpu.VMEM((messages, part, BLOCK), I16),
            pltpu.VMEM((messages, part, BLOCK), I16),
            pltpu.VMEM((messages, 1, BLOCK), F32),
            pltpu.VMEM((messages, 1, BLOCK), F32),
            dma((chips,)), dma((chips,)), dma((chips,)),
            dma((2, messages)), dma((2, messages)), dma((messages,)), dma((messages,)),
            dma((2, messages)), dma((2, messages)), dma((2, messages)), dma((2, messages)),
            dma((2, 3)), dma((2, 3)),
            pltpu.VMEM(loc_tiles.shape, BF16),
            pltpu.VMEM(obs_col.shape, I32),
            pltpu.VMEM(obs_wts.shape, F32),
            pltpu.VMEM(innovation.shape, F32),
            pltpu.VMEM(inv_error.shape, F32),
            pltpu.VMEM((2, per, rows, BLOCK), F32),
            dma((5 + per + 2 * per * PIECES,)),
        ],
        compiler_params=pltpu.CompilerParams(
            collective_id=0, has_side_effects=True, vmem_limit_bytes=58 * 1024 * 1024
        ),
        name="envar_gradients",
    )(
        control, block_lists.T, loc_tiles, ensemble.reshape(slots, rows, cells), obs_col,
        obs_wts, innovation, inv_error,
    )
    base = control.astype(F32)
    first = base + first
    return first, (base - descent_step * first) + second


def solution(mesh):
    placed = (
        P("slot", "space"),
        P("space", None),
        P("space", None, None, None),
        P("slot", None, "space"),
        P("slot", "space"),
        P("slot", None, "space"),
        P("slot", "space"),
        P("slot", "space"),
    )
    return jax.shard_map(
        per_device,
        mesh=mesh,
        in_specs=placed,
        out_specs=(P("slot", "space"), P("slot", "space")),
        check_vma=False,
    )
```

```python
import functools

import jax
import jax.numpy as jnp
from jax import lax
from jax.experimental import pallas as pl
from jax.experimental.pallas import tpu as pltpu
from jax.sharding import PartitionSpec as P

LEV = 48
BLOCK = 128
CORES = 2
OBS_CHUNK = 1024
TOP = 32700.0
descent_step = 0.5
F32 = jnp.float32
BF16 = jnp.bfloat16
I16 = jnp.int16
I32 = jnp.int32
MESH = pl.DeviceIdType.MESH


def halves(x):
    high = x.astype(BF16)
    return high, (x - high.astype(F32)).astype(BF16)


def dot(a, b):
    return lax.dot_general(a, b, (((1,), (0,)), ((), ())), preferred_element_type=F32)


HOP, EXTRA, FLIT = 2.8, 0.5, 1.03
FORCE, MIX, CODE, UNCODE, ROOT, RELAY, FIRST, SECOND, TABLE = 0.45, 0.15, 0.08, 0.03, 0.2, 0.03, 0.7, 1.0, 0.4


def bits_of(m):
    return [1 << i for i in range(m.bit_length()) if m >> i & 1]


PIECES = 1
TREE = ((0, 0, 0, 2, 0, 1, 2, 3, 0, 1, 2, 3, 4, 5, 6, 12), (0, 2, 0, 2, 0, 4, 2, 3, 0, 8, 2, 8, 8, 9, 6, 11))
TREE_UP = ((0, 0, 0, 2, 0, 1, 2, 3, 0, 1, 2, 3, 4, 5, 6, 12), (0, 2, 0, 2, 0, 4, 2, 3, 0, 8, 2, 8, 8, 9, 6, 11))


def tree(spaces, chips, per, table):
    hops, children = {}, {}
    for j in range(per):
        for m in range(spaces):
            for k in range(chips):
                bits = bits_of(m)
                if (spaces, chips, per) == (4, 4, len(table)):
                    above = table[j][m * chips + k]
                    hop = (m ^ above // chips, k ^ above % chips)
                    if not any(hop):
                        continue
                elif k % 2 and (j % 2 or not m):
                    hop = (0, 1)
                elif m:
                    hop = (bits[(len(bits_of(k)) + j) % len(bits)], 0)
                elif k:
                    hop = (0, k)
                else:
                    continue
                hops[m, k, j] = hop
                children.setdefault((m ^ hop[0], k ^ hop[1], j), []).append((m, k, j))
    below = {}

    def height(message):
        if message not in below:
            below[message] = 1 + max([height(child) for child in children.get(message, [])], default=0)
        return below[message]

    for group in children.values():
        group.sort(key=height, reverse=True)
    return hops, children


def arrival(hop, at, links):
    flips, k = hop
    uses = [(bit, FLIT) for bit in bits_of(flips)]
    if k:
        uses.append(("end", FLIT))
    if k > 1:
        uses.append(("middle", 2 * FLIT))
    done = at
    for link, takes in uses:
        at = max(at, links.get(link, 0.0))
        links[link] = at + takes
        done = max(done, links[link])
    return done + HOP + EXTRA * (len(bits_of(flips)) + min(k, 2) - 1)


SALTS = (0, 0, 0)
AMP = 0.15


def ordered(tasks, salt):
    sender = {v: name for name, (_, _, _, sends) in tasks.items() for v, _ in sends}
    hop_of = {v: hop for _, _, _, sends in tasks.values() for v, hop in sends}
    after = {name: [] for name in tasks}
    for name, (_, ends, takes, _) in tasks.items():
        for other in ends:
            after[other].append((name, 0.0))
        for v in takes:
            after[sender[v]].append((name, HOP + FLIT * (1 + (hop_of[v][1] > 1))))
    rest = {}

    def remaining(name):
        if name not in rest:
            rest[name] = tasks[name][0] + max([gap + remaining(v) for v, gap in after[name]], default=0.0)
        return rest[name]

    place = {name: n for n, name in enumerate(tasks)}

    def weight(name):
        shift = ((place[name] + 1) * (salt * 7919 + 104729) % 10007) / 10007 if salt else 0.5
        return remaining(name) * (1.0 + AMP * (shift - 0.5))

    now, links, ended, there, order = 0.0, {}, {}, {}, []
    left = list(tasks)
    while left:
        ready = {}
        for name in left:
            _, ends, takes, _ = tasks[name]
            if all(v in ended for v in ends) and all(v in there for v in takes):
                ready[name] = max([ended[v] for v in ends] + [there[v] for v in takes], default=0.0)
        able = [v for v in ready if ready[v] <= now]
        if not able:
            now = min(ready.values())
            able = [v for v in ready if ready[v] <= now]
        name = max(able, key=weight)
        takes_time, _, _, sends = tasks[name]
        now += takes_time
        ended[name] = now
        for v, hop in sends:
            there[v] = arrival(hop, now, links)
        order.append(name)
        left.remove(name)
    return order


def encode(x, ref, unit):
    top = jnp.max(jnp.abs(x), axis=0, keepdims=True)
    scale = jnp.maximum(top, 1e-30) * (1.0 / TOP)
    unit[...] = scale
    ref[...] = jnp.round(x * (1.0 / scale)).astype(I32).astype(I16)


def decode(ref, unit):
    return ref[...].astype(I32).astype(F32) * unit[...]


def kernel(spaces, slots, *refs):
    chips = slots // CORES
    (control, lists, tiles_hbm, ensemble, cols_hbm, wts_hbm, innovation_hbm, inverse_hbm, first_hbm, second_hbm) = refs[:10]
    ctl, coded, units = (refs[10 + n * chips : 10 + (n + 1) * chips] for n in range(3))
    (
        ens, tiles_t, tiles_a, inv, pick, pick_t, inc, inc_out, inc_in, pair, seen_back, adj, adj_in, split, forced, con,
        rs_out, rs_in, out_unit, in_unit, own_s, ens_s, ens_r, ag_s, ag_r, au_s, au_r, rs_s, rs_r, ru_s, ru_r, x_s, x_r,
        tiles, cols, wts, innovation, inverse, outs, io_s,
    ) = refs[10 + 3 * chips :]
    rows, width = control.shape
    per = width // BLOCK
    cells = ensemble.shape[2]
    nobs = cols.shape[1]
    blocks = cells // BLOCK
    listed = lists.shape[0]
    ncb = spaces * per
    members = rows // LEV
    me = lax.axis_index("space")
    slot = lax.axis_index("slot")
    z, core = slot // CORES, lax.rem(slot, CORES)
    sibling = {"slot": slot + 1 - 2 * core}
    part = rows // PIECES
    hops, children = tree(spaces, chips, per * PIECES, TREE)
    hops_up, children_up = tree(spaces, chips, per * PIECES, TREE_UP)

    def flipped(index, flips):
        at = index
        for bit in bits_of(flips):
            at = at + bit * (1 - 2 * lax.rem(index // bit, 2))
        return at

    def space_at(m):
        return flipped(me, m)

    def device_at(hop):
        where = {}
        if hop[0]:
            where["space"] = flipped(me, hop[0])
        if hop[1]:
            where["slot"] = flipped(z, hop[1]) * CORES + core
        return where

    def number(message):
        m, k, j = message
        return (j * spaces + m) * chips + k

    def fetch(src, dst, n):
        copy = pltpu.make_async_copy(src, dst, io_s.at[n])
        copy.start()
        return copy

    mine = [
        fetch(control.at[:, pl.ds(j * BLOCK, BLOCK)], ctl[0].at[per * me + j], j) for j in range(per)
    ]
    barrier = pltpu.get_barrier_semaphore()
    near = [device_at(hop) for hop in sorted({*hops.values(), *hops_up.values()})] + [sibling]
    for where in near:
        pl.semaphore_signal(barrier, inc=1, device_id=where, device_id_type=MESH)
    loads = ((tiles_hbm, tiles), (cols_hbm, cols), (wts_hbm, wts), (innovation_hbm, innovation), (inverse_hbm, inverse))
    loads = [fetch(src, dst, per + n) for n, (src, dst) in enumerate(loads)]
    for copy in mine:
        copy.wait()
    pl.semaphore_wait(barrier, len(near))

    started = []

    def send(src, dst, ssem, rsem, where):
        copy = pltpu.make_async_remote_copy(
            src_ref=src, dst_ref=dst, send_sem=ssem, recv_sem=rsem,
            device_id=where, device_id_type=MESH,
        )
        copy.start()
        started.append(copy)
        return copy

    gathers = {}

    def kept(i, k, m, j):
        at, r = per * space_at(m) + j % per, j // per
        return (coded if i else ctl)[k].at[at, pl.ds(r * part, part)]

    def unit_of(k, m, j):
        return units[k].at[per * space_at(m) + j % per, j // per]

    def pass_on(i, message):
        m, k, j = message
        for child in children.get(message, []):
            to = number(child)
            where = device_at(hops[child])
            gathers[i, child] = [
                send(kept(i, k, m, j), kept(i, child[1], m, j), ag_s.at[i, to], ag_r.at[i, to], where)
            ]
            if i:
                gathers[i, child].append(
                    send(unit_of(k, m, j), unit_of(child[1], m, j), au_s.at[to], au_r.at[to], where)
                )

    def relay(i, message):
        for copy in gathers[i, message]:
            copy.wait_recv()
        pass_on(i, message)

    for j in range(per * PIECES):
        pass_on(0, (0, 0, j))
    moved = {}
    for k in range(chips):
        there = flipped(z, k) * CORES
        moved[k] = [send(ensemble.at[there + 1 - core], ens.at[1, k], ens_s.at[k], ens_r.at[k], sibling).wait_recv]
        own = pltpu.make_async_copy(ensemble.at[there + core], ens.at[0, k], own_s.at[k])
        own.start()
        moved[k].append(own.wait)

    for copy in loads:
        copy.wait()

    def build_tiles(g, carry):
        for e in range(listed):
            tiles_t[g, e * BLOCK : (e + 1) * BLOCK] = tiles[g, e].astype(F32).T.astype(BF16)
        return carry

    def build_adjoint(b, carry):
        one, two = jnp.int32(-1), jnp.int32(-1)
        for g in range(blocks):
            for e in range(listed):
                hit = lists[e, g] == b
                two = jnp.where(hit, jnp.where(one >= 0, g * listed + e, two), two)
                one = jnp.where(hit, jnp.where(one >= 0, one, g * listed + e), one)
        for place, found in enumerate((one, two)):
            kept = jnp.where(found >= 0, 1.0, 0.0)
            found = jnp.maximum(found, 0)
            g = found // listed
            inv[b, place] = g
            tile = tiles[g, lax.rem(found, listed)].astype(F32) * kept
            tiles_a[b, place * BLOCK : (place + 1) * BLOCK] = tile.astype(BF16)
        return carry

    first_cell = me * cells

    def build_pick(q):
        line = cols[:, q * OBS_CHUNK : (q + 1) * OBS_CHUNK] - first_cell

        def band(r, carry):
            rowid = lax.broadcasted_iota(I32, (BLOCK, OBS_CHUNK), 0) + r * BLOCK
            at = pl.ds(pl.multiple_of(r * BLOCK, BLOCK), BLOCK)
            pick[q, at] = jnp.where(rowid == line, 1.0, 0.0).astype(BF16)
            return carry

        lax.fori_loop(0, blocks, band, 0)
        turned = [
            jnp.broadcast_to(line[:, h * BLOCK : (h + 1) * BLOCK].astype(F32), (BLOCK, BLOCK)).T
            for h in range(OBS_CHUNK // BLOCK)
        ]

        def band_t(r, carry):
            lane = (lax.broadcasted_iota(I32, (BLOCK, BLOCK), 1) + r * BLOCK).astype(F32)
            at = pl.ds(pl.multiple_of(r * BLOCK, BLOCK), BLOCK)
            for h, column in enumerate(turned):
                pick_t[q * OBS_CHUNK + h * BLOCK : q * OBS_CHUNK + (h + 1) * BLOCK, at] = jnp.where(column == lane, 1.0, 0.0).astype(BF16)
            return carry

        lax.fori_loop(0, blocks, band_t, 0)

    def tables_of_tiles():
        lax.fori_loop(0, blocks, build_tiles, 0)

    def tables_of_adjoint():
        lax.fori_loop(0, ncb, build_adjoint, 0)

    def member(n):
        return slice(n * LEV, (n + 1) * LEV)

    def lanes(g):
        return pl.ds(pl.multiple_of(g * BLOCK, BLOCK), BLOCK)

    spread_yet = set()
    swaps = {}

    def spread(i, k):
        fresh = i not in spread_yet
        spread_yet.add(i)
        for m in range(spaces):
            for j in range(per * PIECES):
                if (m or k) and (m, k, j) not in children:
                    for copy in gathers[i, (m, k, j)]:
                        copy.wait_recv()
        if not i:
            for arrive in moved[k]:
                arrive()
        if i:

            def unpack(b, carry):
                for r in range(PIECES):
                    up, down = halves(decode(coded[k].at[b, r * part : (r + 1) * part], units[k].at[b, r]))
                    split[b, r * part : (r + 1) * part] = up
                    split[b, rows + r * part : rows + (r + 1) * part] = down
                return carry

            lax.fori_loop(0, ncb, unpack, 0, unroll=2)

        def run(g, carry):
            held = split if i else ctl[k]
            left = jnp.concatenate([held[lists[e, g]] for e in range(listed)], axis=1)
            value = dot(left, tiles_t[g])
            if i:
                value = value[:rows] + value[rows:]
            at = lanes(g)
            for s, target in enumerate((inc, inc_out.at[i])):
                total = None if fresh else target[:, at]
                for n in range(members):
                    term = ens[s, k, member(n), at].astype(F32) * value[member(n)]
                    total = term if total is None else total + term
                target[:, at] = total
            return carry

        lax.fori_loop(0, blocks, run, 0, unroll=4)

    def observe_all(i):
        earlier = list(started)
        swap = send(inc_out.at[i], inc_in.at[i], x_s.at[i, 0], x_r.at[i, 0], sibling)
        for copy in earlier:
            copy.wait_send()
        started[:] = [swap]
        used.clear()
        swap.wait_recv()
        high, low = halves(inc[...] + inc_in[i])
        pair[:LEV] = high
        pair[LEV:] = low

        def observe(q, carry):
            at = pl.ds(pl.multiple_of(q * OBS_CHUNK, OBS_CHUNK), OBS_CHUNK)
            seen = dot(pair[...], pick[q])
            seen = seen[:LEV] + seen[LEV:]
            w = wts[0, :, at]
            modelled = jnp.sum(w * seen, axis=0, keepdims=True)
            residual = inverse[:, at] * (modelled - innovation[:, at])
            up, down = halves(w * residual)
            seen_back[:LEV, at] = up
            seen_back[LEV:, at] = down
            return carry

        lax.fori_loop(0, nobs // OBS_CHUNK, observe, 0, unroll=True)
        for h in range(2):
            at = slice(h * cells // 2, (h + 1) * cells // 2)
            back = dot(seen_back[...], pick_t[:, at])
            adj[i, h] = back[:LEV] + back[LEV:]
            swaps[i, h] = send(adj.at[i, h], adj_in.at[i, h], x_s.at[i, 1 + h], x_r.at[i, 1 + h], sibling)

    def force(i, k):
        for h in range(2):
            if (i, h) in swaps:
                swaps.pop((i, h)).wait_recv()

            def fill(g, carry):
                at = lanes(g)
                near = pl.ds(pl.multiple_of((g - h * (blocks // 2)) * BLOCK, BLOCK), BLOCK)
                mine, other = adj[i, h, :, near], adj_in[i, h, :, near]
                for n in range(members):
                    total = ens[0, k, member(n), at].astype(F32) * mine + ens[1, k, member(n), at].astype(F32) * other
                    up, down = halves(total)
                    forced[g, member(n)] = up
                    forced[g, rows + n * LEV : rows + (n + 1) * LEV] = down
                return carry

            lax.fori_loop(h * (blocks // 2), (h + 1) * (blocks // 2), fill, 0, unroll=2)

    def mix(k, j):
        def multiply(q, carry):
            b = per * q + j
            left = jnp.concatenate([forced[inv[b, place]] for place in range(2)], axis=1)
            both = dot(left, tiles_a[b])
            con[k, b] = both[:rows] + both[rows:]
            return carry

        lax.fori_loop(0, spaces, multiply, 0, unroll=4)

    sums, used = {}, {}

    def partial(i, message):
        m, k, j = message
        r = j // per
        total = con[k, per * space_at(m) + j % per, r * part : (r + 1) * part]
        for child in children_up.get(message, []):
            for copy in sums[i, child]:
                copy.wait_recv()
            total = total + decode(rs_in.at[number(child)], in_unit.at[number(child)])
        return total

    def pass_up(i, message):
        at = number(message)
        total = partial(i, message)
        if message in used:
            for old in used[message]:
                old.wait_send()
                started[:] = [copy for copy in started if copy is not old]
        encode(total, rs_out.at[at], out_unit.at[at])
        where = device_at(hops_up[message])
        sums[i, message] = used[message] = [
            send(out_unit.at[at], in_unit.at[at], ru_s.at[i, at], ru_r.at[i, at], where),
            send(rs_out.at[at], rs_in.at[at], rs_s.at[i, at], rs_r.at[i, at], where),
        ]

    def root(i, j):
        r, column = j // per, j % per
        band = slice(r * part, (r + 1) * part)
        base = ctl[0][per * me + column, band].astype(F32)
        terms = partial(i, (0, 0, j))
        outs[i, column, band] = terms
        out = (second_hbm if i else first_hbm).at[pl.ds(r * part, part), pl.ds(column * BLOCK, BLOCK)]
        written.append(fetch(outs.at[i, column, pl.ds(r * part, part)], out, per + 5 + i * per * PIECES + j))
        if not i:
            encode(base - descent_step * (base + terms), kept(1, 0, 0, j), unit_of(0, 0, j))
            pass_on(1, (0, 0, j))

    written = []
    far_first = sorted(range(chips), key=lambda k: (-k, k))
    near_first = sorted(range(chips))

    def gathering(i, tasks, roots):
        names = {}
        for message in hops:
            if message in children:
                sends = [((i, child), hops[child]) for child in children[message]]
                tasks[relay, i, message] = (RELAY, [], [(i, message)], sends)
        for k in near_first:
            needs = [(relay, i, (m, k, j)) for m in range(spaces) for j in range(per * PIECES) if (m, k, j) in children and (m or k)]
            takes = [(i, (m, k, j)) for m in range(spaces) for j in range(per * PIECES) if (m, k, j) not in children]
            tasks[spread, i, k] = (SECOND if i else FIRST, needs + roots, takes, [])

    def summing(i, tasks):
        before = []
        for k in far_first:
            tasks[force, i, k] = (FORCE, before, [], [])
            before = []
            for j in range(per):
                tasks[mix, k, j] = (MIX, [(force, i, k)], [], [])
                before.append((mix, k, j))
        for message, hop in hops_up.items():
            takes = [(i, "sum", child) for child in children_up.get(message, [])]
            tasks[pass_up, i, message] = (
                CODE + UNCODE * len(takes), [(mix, message[1], message[2] % per)], takes, [((i, "sum", message), hop)]
            )
        for j in range(per * PIECES):
            takes = [(i, "sum", child) for child in children_up[0, 0, j]]
            sends = [] if i else [((1, child), hops[child]) for child in children[0, 0, j]]
            tasks[root, i, j] = (ROOT, [(mix, 0, j % per)], takes, sends)

    def run(tasks, salt):
        for name in ordered(tasks, salt):
            name[0](*name[1:])

    tables = [(tables_of_tiles,), (tables_of_adjoint,)] + [(build_pick, q) for q in range(nobs // OBS_CHUNK)]
    tasks = {}
    tasks["start",] = (0.0, [], [], [((0, child), hops[child]) for j in range(per * PIECES) for child in children[0, 0, j]])
    for name in tables:
        tasks[name] = (TABLE, [], [], [])
    gathering(0, tasks, [(tables_of_tiles,)])
    for name in ordered(tasks, SALTS[0]):
        if name != ("start",):
            name[0](*name[1:])
    observe_all(0)
    tasks = {}
    summing(0, tasks)
    gathering(1, tasks, [(root, 0, j) for j in range(per * PIECES)])
    run(tasks, SALTS[1])
    observe_all(1)
    tasks = {}
    summing(1, tasks)
    run(tasks, SALTS[2])
    for copy in started:
        copy.wait_send()
    for copy in written:
        copy.wait()


def per_device(control, block_lists, loc_tiles, ensemble, obs_col, obs_wts, innovation, inv_error):
    rows, width = control.shape
    cells = ensemble.shape[2]
    nobs = obs_col.shape[1]
    spaces, slots = lax.axis_size("space"), lax.axis_size("slot")
    chips = slots // CORES
    per = width // BLOCK
    ncb = spaces * per
    blocks = cells // BLOCK
    messages = per * PIECES * spaces * chips
    part = rows // PIECES
    dma = pltpu.SemaphoreType.DMA
    hbm = pl.BlockSpec(memory_space=pl.ANY)
    out = jax.ShapeDtypeStruct((rows, width), F32)
    first, second = pl.pallas_call(
        functools.partial(kernel, spaces, slots),
        out_shape=(out, out),
        in_specs=[
            hbm, pl.BlockSpec(memory_space=pltpu.SMEM), hbm, hbm, hbm, hbm, hbm, hbm,
        ],
        out_specs=(hbm, hbm),
        scratch_shapes=[pltpu.VMEM((ncb, rows, BLOCK), BF16)] * chips
        + [pltpu.VMEM((ncb, rows, BLOCK), I16)] * chips
        + [pltpu.VMEM((ncb, PIECES, 1, BLOCK), F32)] * chips
        + [
            pltpu.VMEM((CORES, chips, rows, cells), BF16),
            pltpu.VMEM((blocks, 2 * BLOCK, BLOCK), BF16),
            pltpu.VMEM((ncb, 2 * BLOCK, BLOCK), BF16),
            pltpu.SMEM((ncb, 2), I32),
            pltpu.VMEM((nobs // OBS_CHUNK, cells, OBS_CHUNK), BF16),
            pltpu.VMEM((nobs, cells), BF16),
            pltpu.VMEM((LEV, cells), F32),
            pltpu.VMEM((2, LEV, cells), F32),
            pltpu.VMEM((2, LEV, cells), F32),
            pltpu.VMEM((2 * LEV, cells), BF16),
            pltpu.VMEM((2 * LEV, nobs), BF16),
            pltpu.VMEM((2, 2, LEV, cells // 2), F32),
            pltpu.VMEM((2, 2, LEV, cells // 2), F32),
            pltpu.VMEM((ncb, 2 * rows, BLOCK), BF16),
            pltpu.VMEM((blocks, 2 * rows, BLOCK), BF16),
            pltpu.VMEM((chips, ncb, rows, BLOCK), F32),
            pltpu.VMEM((messages, part, BLOCK), I16),
            pltpu.VMEM((messages, part, BLOCK), I16),
            pltpu.VMEM((messages, 1, BLOCK), F32),
            pltpu.VMEM((messages, 1, BLOCK), F32),
            dma((chips,)), dma((chips,)), dma((chips,)),
            dma((2, messages)), dma((2, messages)), dma((messages,)), dma((messages,)),
            dma((2, messages)), dma((2, messages)), dma((2, messages)), dma((2, messages)),
            dma((2, 3)), dma((2, 3)),
            pltpu.VMEM(loc_tiles.shape, BF16),
            pltpu.VMEM(obs_col.shape, I32),
            pltpu.VMEM(obs_wts.shape, F32),
            pltpu.VMEM(innovation.shape, F32),
            pltpu.VMEM(inv_error.shape, F32),
            pltpu.VMEM((2, per, rows, BLOCK), F32),
            dma((5 + per + 2 * per * PIECES,)),
        ],
        compiler_params=pltpu.CompilerParams(
            collective_id=0, has_side_effects=True, vmem_limit_bytes=58 * 1024 * 1024
        ),
        name="envar_gradients",
    )(
        control, block_lists.T, loc_tiles, ensemble.reshape(slots, rows, cells), obs_col,
        obs_wts, innovation, inv_error,
    )
    base = control.astype(F32)
    first = base + first
    return first, (base - descent_step * first) + second


def solution(mesh):
    placed = (
        P("slot", "space"),
        P("space", None),
        P("space", None, None, None),
        P("slot", None, "space"),
        P("slot", "space"),
        P("slot", None, "space"),
        P("slot", "space"),
        P("slot", "space"),
    )
    return jax.shard_map(
        per_device,
        mesh=mesh,
        in_specs=placed,
        out_specs=(P("slot", "space"), P("slot", "space")),
        check_vma=False,
    )
```
